128 devices in a mesh: kz: 8 (over x_hi, z), en: 16 (over y, x_lo, core).
Axes of the slice: x: 4 (x_hi: 2, x_lo: 2; x = x_hi * 2 + x_lo), y: 4, z: 4, core: 2. Of those that a mesh axis runs over, the one named last changes fastest.
Arguments:
- green_lesser: bfloat16 [8, 32, 2, 512, 512], P('kz', 'en'), may hold values from -6 to 6
- coupling: float32 [3, 4, 2, 128, 128], replicated, may hold values from -0.25 to 0.25
- block_list: int32 [3, 4, 2], replicated, may hold values from 0 to 3, as said below
- offsets: int32 [3], replicated, may hold values from -1 to 1, as said below
- shifts: int32 [3], replicated, may hold values from 1 to 2, as said below
- occupation: float32 [3], replicated, may hold values from 0.25 to 4
Outputs:
- sigma_lesser: float32 [8, 32, 2, 512, 512], P('kz', 'en')
The draws below stay inside these ranges and needn't reach their ends.
Inputs may be any that keep to these rules, and one draw needn't show every extreme that they name: `block_list`: for each transfer, the 4 listed blocks hold every block row once and every block column once. -1 and +1 each occur among the offsets. 1 and 2 each occur among the shifts.
All inputs are finite; a program needn't handle non-finite values.
Results may differ from the reference program's by a relative error of at most 0.0057.
Values may be sent and summed in bfloat16 or wider, within the bound.
A program may use at most 128 MiB of HBM per device.

```python
import math
import jax
import jax.numpy as jnp
from jax import lax

O = 512
BS = 128
NB = 4
NQ = 3
SMAX = 2
NK = 8
NE = 32


def draw_block_list(key, part):
    transfer_keys = jax.random.split(jax.random.fold_in(key, 101), NQ)

    def draw_single(subkey):
        row_key, column_key = jax.random.split(subkey)
        row_order = jax.random.permutation(row_key, NB)
        column_order = jax.random.permutation(column_key, NB)
        return jnp.stack([row_order, column_order], axis=1).astype(jnp.int32)
    return jax.vmap(draw_single)(transfer_keys)


def draw_offsets(key, part):
    place_key = jax.random.fold_in(key, 202)
    value_key = jax.random.fold_in(key, 203)
    positions = jax.random.permutation(place_key, NQ)
    values = jax.random.randint(value_key, (NQ,), -1, 2)
    values = values.at[positions[0]].set(-1)
    values = values.at[positions[1]].set(1)
    return values.astype(jnp.int32)


def draw_shifts(key, part):
    place_key = jax.random.fold_in(key, 302)
    value_key = jax.random.fold_in(key, 303)
    positions = jax.random.permutation(place_key, NQ)
    values = jax.random.randint(value_key, (NQ,), 1, SMAX + 1)
    values = values.at[positions[0]].set(SMAX)
    values = values.at[positions[1]].set(1)
    return values.astype(jnp.int32)


def block_levels(own_key, extent, pieces, smallest, high):
    gain = 1.0
    for axis_at, shards_of in pieces:
        heights = jax.random.uniform(jax.random.fold_in(jax.random.fold_in(own_key, 6), axis_at), (shards_of,), jnp.float32, smallest / len(pieces), high / len(pieces))
        gain = gain * jnp.repeat(jnp.exp(heights), extent[axis_at] // shards_of).reshape((-1,) + (1,) * (len(extent) - 1 - axis_at))
    return gain


def normal_values(key, dims, width, reach, cuts=(), kind=jnp.bfloat16):
    factor_of = block_levels(key, dims, cuts, -0.22, 0.18) if cuts else 1.0
    array = jax.random.normal(key, dims, jnp.float32) * width * factor_of
    return jnp.minimum(jnp.maximum(array, -reach), reach).astype(kind)


def setup_inputs(seed: int = 0) -> dict:
    key_list = jax.random.split(jax.random.key(seed), 7)
    green_lesser = normal_values(key_list[0], (NK, NE, 2, O, O), 1.0, 6.0, ((0, 8), (1, 16)))
    coupling = normal_values(key_list[1], (NQ, NB, 2, BS, BS), O ** -0.5, 0.25, (), jnp.float32)
    block_list = draw_block_list(jax.random.fold_in(key_list[6], 71), 0)
    offsets = draw_offsets(jax.random.fold_in(key_list[6], 71), 0)
    shifts = draw_shifts(jax.random.fold_in(key_list[6], 71), 0)
    occupation = jnp.clip(jnp.exp(jax.random.uniform(key_list[5], (NQ,), jnp.float32, math.log(0.25), math.log(4.0))), 0.25, 4.0)
    return dict(green_lesser=green_lesser, coupling=coupling, block_list=block_list, offsets=offsets, shifts=shifts, occupation=occupation)


def sandwich(field, blocks, row_index, column_index):
    batch_count = field.shape[0]
    orbitals = field.shape[-1]
    block_size = blocks.shape[-1]
    block_count = orbitals // block_size
    highest = lax.Precision.HIGHEST
    real_part = blocks[:, 0].astype(jnp.float32)
    imag_part = blocks[:, 1].astype(jnp.float32)
    placement = (row_index[:, None] == jnp.arange(block_count, dtype=jnp.int32)[None, :]).astype(jnp.float32)
    row_blocks = field.reshape(batch_count, 2, block_count, block_size, orbitals)
    picked = jnp.take(row_blocks, column_index, axis=2).astype(jnp.float32)

    def product_left(matrix, other):
        return jnp.einsum('nxy,lnyo->lnxo', matrix, other, precision=highest)

    left_real = product_left(real_part, picked[:, 0]) - product_left(imag_part, picked[:, 1])
    left_imag = product_left(real_part, picked[:, 1]) + product_left(imag_part, picked[:, 0])
    products = jnp.stack([left_real, left_imag], axis=1)
    left_half = jnp.einsum('na,lcnxo->lcaxo', placement, products, precision=highest)
    left_half = left_half.reshape(batch_count, 2, orbitals, orbitals).astype(jnp.bfloat16)
    column_blocks = left_half.reshape(batch_count, 2, orbitals, block_count, block_size)
    chosen = jnp.take(column_blocks, column_index, axis=3).astype(jnp.float32)

    def product_right(other, matrix):
        return jnp.einsum('lony,nxy->lonx', other, matrix, precision=highest)

    right_real = product_right(chosen[:, 0], real_part) + product_right(chosen[:, 1], imag_part)
    right_imag = product_right(chosen[:, 1], real_part) - product_right(chosen[:, 0], imag_part)
    stacked = jnp.stack([right_real, right_imag], axis=1)
    result = jnp.einsum('na,lconx->lcoax', placement, stacked, precision=highest)
    return result.reshape(batch_count, 2, orbitals, orbitals)


def reference(green_lesser, coupling, block_list, offsets, shifts, occupation):
    coupling_rounded = coupling.astype(jnp.bfloat16)
    momenta = green_lesser.shape[0]
    energies = green_lesser.shape[1]
    padded = jnp.pad(green_lesser, ((0, 0), (SMAX, SMAX), (0, 0), (0, 0), (0, 0)))

    def one_momentum(momentum):
        sigma_sum = jnp.zeros(green_lesser.shape[1:], jnp.float32)
        for transfer in range(NQ):
            source = jnp.mod(momentum - offsets[transfer], momenta).astype(jnp.int32)
            source_row = lax.dynamic_index_in_dim(padded, source, 0, keepdims=False)
            absorbed = lax.dynamic_slice_in_dim(source_row, (SMAX - shifts[transfer]).astype(jnp.int32), energies, 0)
            emitted = lax.dynamic_slice_in_dim(source_row, (SMAX + shifts[transfer]).astype(jnp.int32), energies, 0)
            weight = occupation[transfer]
            combined = (weight * absorbed.astype(jnp.float32) + (weight + 1.0) * emitted.astype(jnp.float32)).astype(jnp.bfloat16)
            sigma_sum = sigma_sum + sandwich(combined, coupling_rounded[transfer], block_list[transfer, :, 0], block_list[transfer, :, 1])
        return sigma_sum

    return lax.map(one_momentum, jnp.arange(momenta, dtype=jnp.int32))
```

```python
import jax
import jax.numpy as jnp
from jax import lax
from jax.experimental import pallas as pl
from jax.experimental.pallas import tpu as pltpu
from jax.sharding import PartitionSpec as P

MESH = pl.DeviceIdType.MESH
BS = 128
NB = 4
NCH = NB * NB
F32 = jnp.float32
BF16 = jnp.bfloat16


def pick(flags, values):
    *head, chosen = values
    for flag, value in reversed(list(zip(flags, head))):
        chosen = jnp.where(flag, value, chosen)
    return chosen


def exchange(
    g_hbm, cp_hbm, bl, off, sh, occ,
    in_p, in_m, sc_hbm, tab,
    gbuf, cbuf, ring, wl, wr, sc, sp, sm, snd_p, snd_m, tq, tn, ti, tj, tx, tinv,
    lsem, scsem, s1s, s1r, s2s, s2r, s3s, s3r, s4s, s4r, zps, zpr, zms, zmr,
):
    kz = lax.axis_index("kz")
    en = lax.axis_index("en")
    z = kz % 4
    y = en // 4
    lo = (en // 2) % 2
    c = en % 2
    flip = 2 - 4 * lo
    partner = (kz, en + 1 - 2 * c)
    mate = (kz, en + flip)
    has_y = ((c == 1) & (y < 3)) | ((c == 0) & (y > 0))
    yen = (en + 6 * c - 3 + 16) % 16
    ydev = (kz, yen)
    at_top = (z == 3).astype(jnp.int32)
    at_bot = (z == 0).astype(jnp.int32)
    up = ((kz + 1) % 8, en + flip * at_top)
    down = ((kz + 7) % 8, en + flip * at_bot)

    g_copies = []
    for b in range(NCH):
        rows = pl.ds(b // NB * BS, BS)
        columns = pl.ds(b % NB * BS, BS)
        g_copies.append(pltpu.make_async_copy(g_hbm.at[0, :, :, rows, columns], gbuf.at[b], lsem.at[b]))
        g_copies[b].start()
    c_copy = pltpu.make_async_copy(cp_hbm, cbuf, lsem.at[NCH])
    c_copy.start()

    barrier = pltpu.get_barrier_semaphore()
    for dev in (partner, mate, up, down, ydev):
        pl.semaphore_signal(barrier, inc=1, device_id=dev, device_id_type=MESH)

    o0, o1 = off[0], off[1]
    q_up = jnp.where(o0 == 1, 0, jnp.where(o1 == 1, 1, 2))
    q_dn = jnp.where(o0 == -1, 0, jnp.where(o1 == -1, 1, 2))
    q_th = jnp.maximum(3 - q_up - q_dn, 0)
    qs = (q_up, q_dn, q_th)
    x = off[q_th]
    rho = []
    for s, q in enumerate(qs):
        rows = [bl[q, n, 0] for n in range(NB)]
        cols = [bl[q, n, 1] for n in range(NB)]
        dest = []
        for i in range(NB):
            hit = [cols[n] == i for n in range(NB)]
            tq[s * NB + i] = q
            tn[s * NB + i] = pick(hit, range(NB))
            dest.append(pick(hit, rows))
        rho.append(dest)
    inv = [[pick([rho[s][i] == r for i in range(NB)], range(NB)) for r in range(NB)] for s in range(3)]
    for s in range(3):
        for r in range(NB):
            tinv[s * NB + r] = inv[s][r]
    tau = []
    for i in range(NB):
        r = jnp.where(x == 1, rho[0][i], rho[1][i])
        t = pick([r == a for a in range(NB)], inv[2])
        tau.append(jnp.where(x == 0, i, t))
    ci = jnp.int32(0)
    cj = jnp.int32(0)
    start = jnp.int32(0)
    start_k = jnp.int32(0)
    seen = [jnp.bool_(False)] * NCH
    for k in range(NCH):
        ti[k] = ci
        tj[k] = cj
        cur = ci * NB + cj
        seen = [seen[b] | (cur == b) for b in range(NCH)]
        ni = pick([ci == a for a in range(NB)], tau)
        nj = pick([cj == a for a in range(NB)], tau)
        closing = (ni * NB + nj) == start
        tx[k] = jnp.where(closing, start_k, min(k + 1, NCH - 1))
        if k + 1 < NCH:
            free = jnp.int32(NCH - 1)
            for b in reversed(range(NCH - 1)):
                free = jnp.where(seen[b], free, b)
            fi = free // NB
            ci = jnp.where(closing, fi, ni)
            cj = jnp.where(closing, free - fi * NB, nj)
            start = jnp.where(closing, free, start)
            start_k = jnp.where(closing, k + 1, start_k)

    t_own = 1 + 2 * lo
    t_swp = 3 - 2 * lo

    def c_partner(k):
        return pltpu.make_async_remote_copy(
            ring.at[k, t_own], ring.at[k, 2 * lo + 2 * c], s1s.at[k], s1r.at[k], device_id=partner, device_id_type=MESH)

    def c_mate(k):
        return pltpu.make_async_remote_copy(
            ring.at[k, t_own], ring.at[k, t_own], s2s.at[k], s2r.at[k], device_id=mate, device_id_type=MESH)

    def c_relay(k):
        return pltpu.make_async_remote_copy(
            ring.at[k, t_swp], ring.at[k, 2 - 2 * lo + 2 * c], s3s.at[k], s3r.at[k], device_id=partner, device_id_type=MESH)

    def c_y(k):
        return pltpu.make_async_remote_copy(
            ring.at[k, 1 + 2 * c], ring.at[k, 4 - 4 * c], s4s.at[k], s4r.at[k], device_id=ydev, device_id_type=MESH)

    def c_up(k):
        return pltpu.make_async_remote_copy(
            snd_p.at[k], in_p.at[k], zps.at[k], zpr.at[k], device_id=up, device_id_type=MESH)

    def c_down(k):
        return pltpu.make_async_remote_copy(
            snd_m.at[k], in_m.at[k], zms.at[k], zmr.at[k], device_id=down, device_id_type=MESH)

    def r_partner(k):
        pltpu.make_async_remote_copy(
            ring.at[k, t_own], ring.at[k, 2 * lo + 2 - 2 * c], s1s.at[k], s1r.at[k], device_id=partner, device_id_type=MESH).wait_recv()

    def r_mate(k):
        pltpu.make_async_remote_copy(
            ring.at[k, t_own], ring.at[k, t_swp], s2s.at[k], s2r.at[k], device_id=mate, device_id_type=MESH).wait_recv()

    def r_relay(k):
        pltpu.make_async_remote_copy(
            ring.at[k, t_swp], ring.at[k, 4 - 2 * lo - 2 * c], s3s.at[k], s3r.at[k], device_id=partner, device_id_type=MESH).wait_recv()

    def r_y(k):
        pltpu.make_async_remote_copy(
            ring.at[k, 1 + 2 * c], ring.at[k, 4 * c], s4s.at[k], s4r.at[k], device_id=ydev, device_id_type=MESH).wait_recv()

    def c_sc(k):
        return pltpu.make_async_copy(sc.at[k], sc_hbm.at[k], scsem.at[k])

    for copy in g_copies:
        copy.wait()
    pl.semaphore_wait(barrier, 5)

    @pl.loop(0, NCH)
    def _(k):
        ring[k, t_own] = gbuf[ti[k] * NB + tj[k]]
        c_mate(k).start()
        c_partner(k).start()

    c_copy.wait()

    @pl.loop(0, 3 * NB)
    def _(a):
        block = cbuf[tq[a], tn[a]]
        real, imag = block[0], block[1]
        rb, ib = real.astype(BF16), imag.astype(BF16)
        wl[a, 0:BS, 0:BS] = rb
        wl[a, 0:BS, BS:2 * BS] = -ib
        wl[a, BS:2 * BS, 0:BS] = ib
        wl[a, BS:2 * BS, BS:2 * BS] = rb
        rt, it = real.T.astype(BF16), imag.T.astype(BF16)
        wr[a, 0:BS, 0:BS] = rt
        wr[a, 0:BS, BS:2 * BS] = -it
        wr[a, BS:2 * BS, 0:BS] = it
        wr[a, BS:2 * BS, BS:2 * BS] = rt

    @pl.when(jnp.logical_not(has_y))
    def _():
        @pl.loop(0, NCH)
        def _(k):
            ring[k, 4 * c] = jnp.zeros((2, 2, BS, BS), BF16)

    def relay(k):
        r_mate(k)
        c_relay(k).start()

        @pl.when(has_y)
        def _():
            c_y(k).start()

    relay(0)
    t_up = jnp.where(z == 3, t_swp, t_own)
    t_dn = jnp.where(z == 0, t_swp, t_own)
    w_up = (x == 1).astype(F32)
    w_dn = (x == -1).astype(F32)
    th_swp = ((x == 1) & (z == 3)) | ((x == -1) & (z == 0))

    def sandwich(k, s, six):
        q = qs[s]
        one = sh[q] == 1
        weight = occ[q]
        cols = []
        for e in range(2):
            low = jnp.where(one, six[e + 1], six[e])
            high = jnp.where(one, six[e + 3], six[e + 4])
            mixed = (weight * low.astype(F32) + (weight + 1.0) * high.astype(F32)).astype(BF16)
            cols.append(mixed.reshape(2 * BS, BS))
        field = jnp.concatenate(cols, axis=1)
        left = jnp.dot(wl[s * NB + ti[k]], field, preferred_element_type=F32).astype(BF16)
        top = jnp.concatenate([left[:BS, :BS], left[BS:, :BS]], axis=1)
        bottom = jnp.concatenate([left[:BS, BS:], left[BS:, BS:]], axis=1)
        return jnp.dot(jnp.concatenate([top, bottom], axis=0), wr[s * NB + tj[k]], preferred_element_type=F32)

    def window(k, t):
        return [ring[k, t - 1 + e // 2, e % 2] for e in range(6)]

    def ship(k):
        third = sc[tx[k]]
        snd_p[k] = (sp[...] + w_up * third).astype(BF16)
        snd_m[k] = (sm[...] + w_dn * third).astype(BF16)
        c_up(k).start()
        c_down(k).start()

    @pl.loop(0, NCH)
    def _(k):
        @pl.when(k + 1 < NCH)
        def _():
            relay(k + 1)

        r_partner(k)
        r_relay(k)

        @pl.when(has_y)
        def _():
            r_y(k)

        own = window(k, t_own)
        swp = window(k, t_swp)
        sc[k] = sandwich(k, 2, [jnp.where(th_swp, b, a) for a, b in zip(own, swp)])
        c_sc(k).start()

        @pl.when(k > 0)
        def _():
            ship(k - 1)

        sp[...] = sandwich(k, 0, window(k, t_up))
        sm[...] = sandwich(k, 1, window(k, t_dn))

    ship(NCH - 1)

    @pl.loop(0, NCH)
    def _(d):
        for s in range(3):
            i = tinv[s * NB + d // NB]
            j = tinv[s * NB + d % NB]
            place = 0
            for k in range(NCH):
                place = jnp.where((ti[k] == i) & (tj[k] == j), k, place)
            if s == 2:
                place = jnp.where(x == 0, place, 0)
            tab[s * NCH + d] = place
    tab[3 * NCH] = (x == 0).astype(jnp.int32)

    @pl.loop(0, NCH)
    def _(k):
        c_partner(k).wait_send()
        c_mate(k).wait_send()
        c_relay(k).wait_send()

        @pl.when(has_y)
        def _():
            c_y(k).wait_send()

        c_sc(k).wait()
        c_up(k).wait()
        c_down(k).wait()


def gather_sum(tab, *refs):
    out = refs[-1]
    keep = tab[3 * NCH].astype(F32)
    for j in range(NB):
        total = refs[j][0].astype(F32) + refs[NB + j][0].astype(F32) + keep * refs[2 * NB + j][0]
        for e in range(2):
            for ri in range(2):
                out[0, e, ri, :, j * BS:(j + 1) * BS] = total[e * BS:(e + 1) * BS, ri * BS:(ri + 1) * BS]


def on_device(green_lesser, coupling, block_list, offsets, shifts, occupation):
    any_spec = pl.BlockSpec(memory_space=pl.ANY)
    smem = pl.BlockSpec(memory_space=pltpu.SMEM)
    dma = pltpu.SemaphoreType.DMA
    chunk = (NCH, 2 * BS, 2 * BS)
    in_p, in_m, third, tab = pl.pallas_call(
        exchange,
        out_shape=(
            jax.ShapeDtypeStruct(chunk, BF16),
            jax.ShapeDtypeStruct(chunk, BF16),
            jax.ShapeDtypeStruct(chunk, F32),
            jax.ShapeDtypeStruct((4 * NCH,), jnp.int32),
        ),
        in_specs=[any_spec, any_spec, smem, smem, smem, smem],
        out_specs=(any_spec, any_spec, any_spec, smem),
        scratch_shapes=[
            pltpu.VMEM((NCH, 2, 2, BS, BS), BF16),
            pltpu.VMEM((3, NB, 2, BS, BS), F32),
            pltpu.VMEM((NCH, 5, 2, 2, BS, BS), BF16),
            pltpu.VMEM((3 * NB, 2 * BS, 2 * BS), BF16),
            pltpu.VMEM((3 * NB, 2 * BS, 2 * BS), BF16),
            pltpu.VMEM(chunk, F32),
            pltpu.VMEM((2 * BS, 2 * BS), F32),
            pltpu.VMEM((2 * BS, 2 * BS), F32),
            pltpu.VMEM(chunk, BF16),
            pltpu.VMEM(chunk, BF16),
            pltpu.SMEM((3 * NB,), jnp.int32),
            pltpu.SMEM((3 * NB,), jnp.int32),
            pltpu.SMEM((NCH,), jnp.int32),
            pltpu.SMEM((NCH,), jnp.int32),
            pltpu.SMEM((NCH,), jnp.int32),
            pltpu.SMEM((3 * NB,), jnp.int32),
            dma((NCH + 1,)),
        ] + [dma((NCH,))] * 13,
        compiler_params=pltpu.CompilerParams(
            collective_id=0, has_side_effects=True, vmem_limit_bytes=56 * 1024 * 1024),
        name="exchange",
    )(green_lesser, coupling, block_list, offsets, shifts, occupation)

    def spec(s, j):
        return pl.BlockSpec((1, 2 * BS, 2 * BS), lambda r, t: (t[s * NCH + r * NB + j], 0, 0))

    return pl.pallas_call(
        gather_sum,
        out_shape=jax.ShapeDtypeStruct(green_lesser.shape, F32),
        grid_spec=pltpu.PrefetchScalarGridSpec(
            num_scalar_prefetch=1,
            grid=(NB,),
            in_specs=[spec(s, j) for s in range(3) for j in range(NB)],
            out_specs=pl.BlockSpec((1, 2, 2, BS, 512), lambda r, t: (0, 0, 0, r, 0)),
        ),
        name="gather_sum",
    )(tab, *([in_p] * NB + [in_m] * NB + [third] * NB))


def solution(mesh):
    placed = (P("kz", "en", None, None, None), P(), P(), P(), P(), P())
    return jax.shard_map(
        on_device,
        mesh=mesh,
        in_specs=placed,
        out_specs=P("kz", "en", None, None, None),
        check_vma=False,
    )
```

```python
import jax
import jax.numpy as jnp
from jax import lax
from jax.experimental import pallas as pl
from jax.experimental.pallas import tpu as pltpu
from jax.sharding import PartitionSpec as P

MESH = pl.DeviceIdType.MESH
BS = 128
NB = 4
NCH = NB * NB
F32 = jnp.float32
BF16 = jnp.bfloat16


def pick(flags, values):
    *head, chosen = values
    for flag, value in reversed(list(zip(flags, head))):
        chosen = jnp.where(flag, value, chosen)
    return chosen


def exchange(
    g_hbm, cp_hbm, bl_hbm, off_hbm, sh_hbm, occ_hbm,
    in_p, in_m, sc, tab,
    gbuf, cbuf, ring, wl, wr, sp, sm, snd_p, snd_m, bl, off, sh, occ, tq, tn, ti, tj, tx, tinv,
    lsem, isem, s1s, s1r, s2s, s2r, s3s, s3r, s4s, s4r, zps, zpr, zms, zmr,
):
    kz = lax.axis_index("kz")
    en = lax.axis_index("en")
    z = kz % 4
    y = en // 4
    lo = (en // 2) % 2
    c = en % 2
    flip = 2 - 4 * lo
    partner = (kz, en + 1 - 2 * c)
    mate = (kz, en + flip)
    has_y = ((c == 1) & (y < 3)) | ((c == 0) & (y > 0))
    yen = (en + 6 * c - 3 + 16) % 16
    ydev = (kz, yen)
    at_top = (z == 3).astype(jnp.int32)
    at_bot = (z == 0).astype(jnp.int32)
    up = ((kz + 1) % 8, en + flip * at_top)
    down = ((kz + 7) % 8, en + flip * at_bot)

    t_own = 1 + 2 * lo
    t_swp = 3 - 2 * lo
    barrier = pltpu.get_barrier_semaphore()
    for dev in (partner, mate, up, down, ydev):
        pl.semaphore_signal(barrier, inc=1, device_id=dev, device_id_type=MESH)
    g_copies = []
    for b in range(NCH):
        rows = pl.ds(b // NB * BS, BS)
        columns = pl.ds(b % NB * BS, BS)
        target = ring.at[0, t_own] if b == 0 else gbuf.at[b]
        g_copies.append(pltpu.make_async_copy(g_hbm.at[0, :, :, rows, columns], target, lsem.at[b]))
        g_copies[b].start()
    small = [
        pltpu.make_async_copy(source, target, isem.at[n])
        for n, (source, target) in enumerate(((bl_hbm, bl), (off_hbm, off), (sh_hbm, sh), (occ_hbm, occ)))
    ]
    for copy in small:
        copy.start()
    c_copy = pltpu.make_async_copy(cp_hbm, cbuf, lsem.at[NCH])
    c_copy.start()

    def c_partner(k):
        return pltpu.make_async_remote_copy(
            ring.at[k, t_own], ring.at[k, 2 * lo + 2 * c], s1s.at[k], s1r.at[k], device_id=partner, device_id_type=MESH)

    def c_mate(k):
        return pltpu.make_async_remote_copy(
            ring.at[k, t_own], ring.at[k, t_own], s2s.at[k], s2r.at[k], device_id=mate, device_id_type=MESH)

    def c_relay(k):
        return pltpu.make_async_remote_copy(
            ring.at[k, t_swp], ring.at[k, 2 - 2 * lo + 2 * c], s3s.at[k], s3r.at[k], device_id=partner, device_id_type=MESH)

    def c_y(k):
        return pltpu.make_async_remote_copy(
            ring.at[k, 1 + 2 * c], ring.at[k, 4 - 4 * c], s4s.at[k], s4r.at[k], device_id=ydev, device_id_type=MESH)

    def c_up(k):
        return pltpu.make_async_remote_copy(
            snd_p.at[k], in_p.at[k], zps.at[k], zpr.at[k], device_id=up, device_id_type=MESH)

    def c_down(k):
        return pltpu.make_async_remote_copy(
            snd_m.at[k], in_m.at[k], zms.at[k], zmr.at[k], device_id=down, device_id_type=MESH)

    def r_partner(k):
        pltpu.make_async_remote_copy(
            ring.at[k, t_own], ring.at[k, 2 * lo + 2 - 2 * c], s1s.at[k], s1r.at[k], device_id=partner, device_id_type=MESH).wait_recv()

    def r_mate(k):
        pltpu.make_async_remote_copy(
            ring.at[k, t_own], ring.at[k, t_swp], s2s.at[k], s2r.at[k], device_id=mate, device_id_type=MESH).wait_recv()

    def r_relay(k):
        pltpu.make_async_remote_copy(
            ring.at[k, t_swp], ring.at[k, 4 - 2 * lo - 2 * c], s3s.at[k], s3r.at[k], device_id=partner, device_id_type=MESH).wait_recv()

    def r_y(k):
        pltpu.make_async_remote_copy(
            ring.at[k, 1 + 2 * c], ring.at[k, 4 * c], s4s.at[k], s4r.at[k], device_id=ydev, device_id_type=MESH).wait_recv()

    g_copies[0].wait()
    pl.semaphore_wait(barrier, 5)
    c_mate(0).start()
    c_partner(0).start()
    for copy in small:
        copy.wait()

    o0, o1 = off[0], off[1]
    q_up = jnp.where(o0 == 1, 0, jnp.where(o1 == 1, 1, 2))
    q_dn = jnp.where(o0 == -1, 0, jnp.where(o1 == -1, 1, 2))
    q_th = jnp.maximum(3 - q_up - q_dn, 0)
    qs = (q_up, q_dn, q_th)
    x = off[q_th]
    rho = []
    for s, q in enumerate(qs):
        rows = [bl[q, 0, n] for n in range(NB)]
        cols = [bl[q, 1, n] for n in range(NB)]
        dest = []
        for i in range(NB):
            hit = [cols[n] == i for n in range(NB)]
            tq[s * NB + i] = q
            tn[s * NB + i] = pick(hit, range(NB))
            dest.append(pick(hit, rows))
        rho.append(dest)
    inv = [[pick([rho[s][i] == r for i in range(NB)], range(NB)) for r in range(NB)] for s in range(3)]
    for s in range(3):
        for r in range(NB):
            tinv[s * NB + r] = inv[s][r]
    tau = []
    for i in range(NB):
        r = jnp.where(x == 1, rho[0][i], rho[1][i])
        t = pick([r == a for a in range(NB)], inv[2])
        tau.append(jnp.where(x == 0, i, t))
    ci = jnp.int32(0)
    cj = jnp.int32(0)
    start = jnp.int32(0)
    start_k = jnp.int32(0)
    seen = [jnp.bool_(False)] * NCH
    for k in range(NCH):
        ti[k] = ci
        tj[k] = cj
        cur = ci * NB + cj
        seen = [seen[b] | (cur == b) for b in range(NCH)]
        ni = pick([ci == a for a in range(NB)], tau)
        nj = pick([cj == a for a in range(NB)], tau)
        closing = (ni * NB + nj) == start
        tx[k] = jnp.where(closing, start_k, min(k + 1, NCH - 1))
        if k + 1 < NCH:
            free = jnp.int32(NCH - 1)
            for b in reversed(range(NCH - 1)):
                free = jnp.where(seen[b], free, b)
            fi = free // NB
            ci = jnp.where(closing, fi, ni)
            cj = jnp.where(closing, free - fi * NB, nj)
            start = jnp.where(closing, free, start)
            start_k = jnp.where(closing, k + 1, start_k)

    for copy in g_copies[1:]:
        copy.wait()

    @pl.loop(1, NCH)
    def _(k):
        ring[k, t_own] = gbuf[ti[k] * NB + tj[k]]
        c_mate(k).start()
        c_partner(k).start()

    c_copy.wait()

    @pl.loop(0, 3 * NB)
    def _(a):
        block = cbuf[tq[a], tn[a]]
        real, imag = block[0], block[1]
        rb, ib = real.astype(BF16), imag.astype(BF16)
        wl[a, 0:BS, 0:BS] = rb
        wl[a, 0:BS, BS:2 * BS] = -ib
        wl[a, BS:2 * BS, 0:BS] = ib
        wl[a, BS:2 * BS, BS:2 * BS] = rb
        rt, it = real.T.astype(BF16), imag.T.astype(BF16)
        wr[a, 0:BS, 0:BS] = rt
        wr[a, 0:BS, BS:2 * BS] = -it
        wr[a, BS:2 * BS, 0:BS] = it
        wr[a, BS:2 * BS, BS:2 * BS] = rt

    @pl.when(jnp.logical_not(has_y))
    def _():
        @pl.loop(0, NCH)
        def _(k):
            ring[k, 4 * c] = jnp.zeros((2, 2, BS, BS), BF16)

    def relay(k):
        r_mate(k)
        c_relay(k).start()

        @pl.when(has_y)
        def _():
            c_y(k).start()

    relay(0)
    t_up = jnp.where(z == 3, t_swp, t_own)
    t_dn = jnp.where(z == 0, t_swp, t_own)
    w_up = (x == 1).astype(F32)
    w_dn = (x == -1).astype(F32)
    th_swp = ((x == 1) & (z == 3)) | ((x == -1) & (z == 0))

    def sandwich(k, s, six):
        q = qs[s]
        one = sh[q] == 1
        weight = occ[q]
        cols = []
        for e in range(2):
            low = jnp.where(one, six[e + 1], six[e])
            high = jnp.where(one, six[e + 3], six[e + 4])
            mixed = (weight * low.astype(F32) + (weight + 1.0) * high.astype(F32)).astype(BF16)
            cols.append(mixed.reshape(2 * BS, BS))
        field = jnp.concatenate(cols, axis=1)
        left = jnp.dot(wl[s * NB + ti[k]], field, preferred_element_type=F32).astype(BF16)
        top = jnp.concatenate([left[:BS, :BS], left[BS:, :BS]], axis=1)
        bottom = jnp.concatenate([left[:BS, BS:], left[BS:, BS:]], axis=1)
        return jnp.dot(jnp.concatenate([top, bottom], axis=0), wr[s * NB + tj[k]], preferred_element_type=F32)

    def window(k, t):
        return [ring[k, t - 1 + e // 2, e % 2] for e in range(6)]

    def ship(k):
        third = sc[tx[k]]
        snd_p[k] = (sp[...] + w_up * third).astype(BF16)
        snd_m[k] = (sm[...] + w_dn * third).astype(BF16)
        c_up(k).start()
        c_down(k).start()

    @pl.loop(0, NCH)
    def _(k):
        @pl.when(k + 1 < NCH)
        def _():
            relay(k + 1)

        r_partner(k)
        r_relay(k)

        @pl.when(has_y)
        def _():
            r_y(k)

        own = window(k, t_own)
        swp = window(k, t_swp)
        sc[k] = sandwich(k, 2, [jnp.where(th_swp, b, a) for a, b in zip(own, swp)])

        @pl.when(k > 0)
        def _():
            ship(k - 1)

        sp[...] = sandwich(k, 0, window(k, t_up))
        sm[...] = sandwich(k, 1, window(k, t_dn))

    ship(NCH - 1)

    @pl.loop(0, NCH)
    def _(d):
        for s in range(3):
            i = tinv[s * NB + d // NB]
            j = tinv[s * NB + d % NB]
            place = 0
            for k in range(NCH):
                place = jnp.where((ti[k] == i) & (tj[k] == j), k, place)
            if s == 2:
                place = jnp.where(x == 0, place, 0)
            tab[s * NCH + d] = place
    tab[3 * NCH] = (x == 0).astype(jnp.int32)

    @pl.loop(0, NCH)
    def _(k):
        c_partner(k).wait_send()
        c_mate(k).wait_send()
        c_relay(k).wait_send()

        @pl.when(has_y)
        def _():
            c_y(k).wait_send()

        c_up(k).wait_send()
        c_down(k).wait_send()

    @pl.loop(0, NCH)
    def _(k):
        c_up(k).wait_recv()
        c_down(k).wait_recv()


def gather_sum(tab, in_p, in_m, third, out, rows, sem):
    def copy(r):
        return pltpu.make_async_copy(rows.at[r], out.at[0, :, :, pl.ds(r * BS, BS), :], sem.at[r])

    def fill(own):
        for r in range(NB):
            for j in range(NB):
                d = r * NB + j
                total = in_p[tab[d]].astype(F32) + in_m[tab[NCH + d]].astype(F32)
                if own:
                    total = total + third[tab[2 * NCH + d]]
                for e in range(2):
                    for ri in range(2):
                        rows[r, e, ri, :, j * BS:(j + 1) * BS] = total[e * BS:(e + 1) * BS, ri * BS:(ri + 1) * BS]
            copy(r).start()

    @pl.when(tab[3 * NCH] == 1)
    def _():
        fill(True)

    @pl.when(tab[3 * NCH] != 1)
    def _():
        fill(False)

    for r in range(NB):
        copy(r).wait()


def on_device(green_lesser, coupling, block_list, offsets, shifts, occupation):
    any_spec = pl.BlockSpec(memory_space=pl.ANY)
    hbm = pl.BlockSpec(memory_space=pltpu.HBM)
    smem = pl.BlockSpec(memory_space=pltpu.SMEM)
    vmem = pl.BlockSpec(memory_space=pltpu.VMEM)
    dma = pltpu.SemaphoreType.DMA
    chunk = (NCH, 2 * BS, 2 * BS)
    in_p, in_m, third, tab = pl.pallas_call(
        exchange,
        out_shape=(
            pltpu.VMEM(chunk, BF16),
            pltpu.VMEM(chunk, BF16),
            pltpu.VMEM(chunk, F32),
            pltpu.SMEM((4 * NCH,), jnp.int32),
        ),
        in_specs=[hbm] * 6,
        out_specs=(vmem, vmem, vmem, smem),
        scratch_shapes=[
            pltpu.VMEM((NCH, 2, 2, BS, BS), BF16),
            pltpu.VMEM((3, NB, 2, BS, BS), F32),
            pltpu.VMEM((NCH, 5, 2, 2, BS, BS), BF16),
            pltpu.VMEM((3 * NB, 2 * BS, 2 * BS), BF16),
            pltpu.VMEM((3 * NB, 2 * BS, 2 * BS), BF16),
            pltpu.VMEM((2 * BS, 2 * BS), F32),
            pltpu.VMEM((2 * BS, 2 * BS), F32),
            pltpu.VMEM(chunk, BF16),
            pltpu.VMEM(chunk, BF16),
            pltpu.SMEM((3, 2, NB), jnp.int32),
            pltpu.SMEM((3,), jnp.int32),
            pltpu.SMEM((3,), jnp.int32),
            pltpu.SMEM((3,), F32),
            pltpu.SMEM((3 * NB,), jnp.int32),
            pltpu.SMEM((3 * NB,), jnp.int32),
            pltpu.SMEM((NCH,), jnp.int32),
            pltpu.SMEM((NCH,), jnp.int32),
            pltpu.SMEM((NCH,), jnp.int32),
            pltpu.SMEM((3 * NB,), jnp.int32),
            dma((NCH + 1,)),
            dma((4,)),
        ] + [dma((NCH,))] * 12,
        compiler_params=pltpu.CompilerParams(
            collective_id=0, has_side_effects=True, vmem_limit_bytes=32 * 1024 * 1024),
        name="exchange",
    )(*(
        pltpu.with_memory_space_constraint(x, pltpu.HBM)
        for x in (green_lesser, coupling, block_list.transpose(0, 2, 1), offsets, shifts, occupation)
    ))
    return pl.pallas_call(
        gather_sum,
        out_shape=jax.ShapeDtypeStruct(green_lesser.shape, F32),
        in_specs=[smem, vmem, vmem, vmem],
        out_specs=any_spec,
        scratch_shapes=[pltpu.VMEM((NB, 2, 2, BS, 512), F32), dma((NB,))],
        compiler_params=pltpu.CompilerParams(vmem_limit_bytes=16 * 1024 * 1024),
        name="gather_sum",
    )(tab, in_p, in_m, third)


def solution(mesh):
    placed = (P("kz", "en", None, None, None), P(), P(), P(), P(), P())
    return jax.shard_map(
        on_device,
        mesh=mesh,
        in_specs=placed,
        out_specs=P("kz", "en", None, None, None),
        check_vma=False,
    )
```

```python
import jax
import jax.numpy as jnp
from jax import lax
from jax.experimental import pallas as pl
from jax.experimental.pallas import tpu as pltpu
from jax.sharding import PartitionSpec as P

MESH = pl.DeviceIdType.MESH
BS = 128
NB = 4
NCH = NB * NB
F32 = jnp.float32
BF16 = jnp.bfloat16


def pick(flags, values):
    *head, chosen = values
    for flag, value in reversed(list(zip(flags, head))):
        chosen = jnp.where(flag, value, chosen)
    return chosen


def exchange(
    g_hbm, cp_hbm, bl_hbm, off_hbm, sh_hbm, occ_hbm,
    in_p, in_m, sc, tab,
    gbuf, cbuf, ring, wl, wr, sp, sm, snd_p, snd_m, bl, off, sh, occ, tq, tn, ti, tj, tx, tinv,
    lsem, isem, sent, got, s1r, s2r, s3r, s4r,
):
    kz = lax.axis_index("kz")
    en = lax.axis_index("en")
    z = kz % 4
    y = en // 4
    lo = (en // 2) % 2
    c = en % 2
    flip = 2 - 4 * lo
    partner = (kz, en + 1 - 2 * c)
    mate = (kz, en + flip)
    has_y = ((c == 1) & (y < 3)) | ((c == 0) & (y > 0))
    yen = (en + 6 * c - 3 + 16) % 16
    ydev = (kz, yen)
    at_top = (z == 3).astype(jnp.int32)
    at_bot = (z == 0).astype(jnp.int32)
    up = ((kz + 1) % 8, en + flip * at_top)
    down = ((kz + 7) % 8, en + flip * at_bot)

    t_own = 1 + 2 * lo
    t_swp = 3 - 2 * lo
    def g_copy(b):
        rows = pl.ds(b // NB * BS, BS)
        columns = pl.ds(b % NB * BS, BS)
        target = ring.at[0, t_own] if b == 0 else gbuf.at[b]
        return pltpu.make_async_copy(g_hbm.at[0, :, :, rows, columns], target, lsem.at[min(b, 1)])

    g_copy(0).start()
    barrier = pltpu.get_barrier_semaphore()
    for dev in (up, down, ydev, mate, partner):
        pl.semaphore_signal(barrier, inc=1, device_id=dev, device_id_type=MESH)
    small = [
        pltpu.make_async_copy(source, target, isem.at[n])
        for n, (source, target) in enumerate(((bl_hbm, bl), (off_hbm, off), (sh_hbm, sh), (occ_hbm, occ)))
    ]
    for copy in small:
        copy.start()
    c_copy = pltpu.make_async_copy(cp_hbm, cbuf, lsem.at[2])

    def c_partner(k, sem):
        return pltpu.make_async_remote_copy(
            ring.at[k, t_own], ring.at[k, 2 * lo + 2 * c], sent.at[0], s1r.at[sem],
            device_id=partner, device_id_type=MESH)

    def c_mate(k):
        return pltpu.make_async_remote_copy(
            ring.at[k, t_own], ring.at[k, t_own], sent.at[1], s2r.at[k], device_id=mate, device_id_type=MESH)

    def c_relay(k):
        return pltpu.make_async_remote_copy(
            ring.at[k, t_swp], ring.at[k, 2 - 2 * lo + 2 * c], sent.at[2], s3r.at[k],
            device_id=partner, device_id_type=MESH)

    def c_y(k):
        return pltpu.make_async_remote_copy(
            ring.at[k, 1 + 2 * c], ring.at[k, 4 - 4 * c], sent.at[3], s4r.at[k], device_id=ydev, device_id_type=MESH)

    def c_up(k):
        return pltpu.make_async_remote_copy(
            snd_p.at[k], in_p.at[k], sent.at[4], got.at[0], device_id=up, device_id_type=MESH)

    def c_down(k):
        return pltpu.make_async_remote_copy(
            snd_m.at[k], in_m.at[k], sent.at[5], got.at[1], device_id=down, device_id_type=MESH)

    def arrived(target, sem, device):
        pltpu.make_async_remote_copy(
            target, target, sent.at[0], sem, device_id=device, device_id_type=MESH).wait_recv()

    def r_mate(k):
        arrived(ring.at[k, t_swp], s2r.at[k], mate)

    def r_relay(k):
        arrived(ring.at[k, 4 - 2 * lo - 2 * c], s3r.at[k], partner)

    def r_y(k):
        arrived(ring.at[k, 4 * c], s4r.at[k], ydev)

    t_partner = 2 * lo + 2 - 2 * c
    y_own = has_y & (lo == c)
    y_relay = has_y & (lo != c)

    def send_mate(k):
        c_mate(k).start()

    def send_chip(k, sem):
        c_partner(k, sem).start()

        @pl.when(y_own)
        def _():
            c_y(k).start()

    g_copy(0).wait()
    pl.semaphore_wait(barrier, 5)
    send_mate(0)
    send_chip(0, 0)
    for b in range(1, NCH):
        g_copy(b).start()
    c_copy.start()
    for copy in small:
        copy.wait()

    o0, o1 = off[0], off[1]
    q_up = jnp.where(o0 == 1, 0, jnp.where(o1 == 1, 1, 2))
    q_dn = jnp.where(o0 == -1, 0, jnp.where(o1 == -1, 1, 2))
    q_th = jnp.maximum(3 - q_up - q_dn, 0)
    qs = (q_up, q_dn, q_th)
    x = off[q_th]
    rho = []
    for s, q in enumerate(qs):
        rows = [bl[q, 0, n] for n in range(NB)]
        cols = [bl[q, 1, n] for n in range(NB)]
        dest = []
        for i in range(NB):
            hit = [cols[n] == i for n in range(NB)]
            tq[s * NB + i] = q
            tn[s * NB + i] = pick(hit, range(NB))
            dest.append(pick(hit, rows))
        rho.append(dest)
    inv = [[pick([rho[s][i] == r for i in range(NB)], range(NB)) for r in range(NB)] for s in range(3)]
    for s in range(3):
        for r in range(NB):
            tinv[s * NB + r] = inv[s][r]
    tau = []
    for i in range(NB):
        r = jnp.where(x == 1, rho[0][i], rho[1][i])
        t = pick([r == a for a in range(NB)], inv[2])
        tau.append(jnp.where(x == 0, i, t))
    ci = jnp.int32(0)
    cj = jnp.int32(0)
    start = jnp.int32(0)
    start_k = jnp.int32(0)
    seen = [jnp.bool_(False)] * NCH
    for k in range(NCH):
        ti[k] = ci
        tj[k] = cj
        cur = ci * NB + cj
        seen = [seen[b] | (cur == b) for b in range(NCH)]
        ni = pick([ci == a for a in range(NB)], tau)
        nj = pick([cj == a for a in range(NB)], tau)
        closing = (ni * NB + nj) == start
        tx[k] = jnp.where(closing, start_k, min(k + 1, NCH - 1))
        if k + 1 < NCH:
            free = jnp.int32(NCH - 1)
            for b in reversed(range(NCH - 1)):
                free = jnp.where(seen[b], free, b)
            fi = free // NB
            ci = jnp.where(closing, fi, ni)
            cj = jnp.where(closing, free - fi * NB, nj)
            start = jnp.where(closing, free, start)
            start_k = jnp.where(closing, k + 1, start_k)

    others = gbuf.at[pl.ds(1, NCH - 1)]
    pltpu.make_async_copy(others, others, lsem.at[1]).wait()

    @pl.loop(1, NCH)
    def _(k):
        ring[k, t_own] = gbuf[ti[k] * NB + tj[k]]

        @pl.when(lo == c)
        def _():
            send_mate(k)

        send_chip(k, 1)

    arrived(ring.at[0, t_partner], s1r.at[0], partner)
    arrived(ring.at[pl.ds(1, NCH - 1), t_partner], s1r.at[1], partner)

    @pl.when(lo != c)
    def _():
        @pl.loop(1, NCH)
        def _(k):
            send_mate(k)

    c_copy.wait()

    @pl.loop(0, 3 * NB)
    def _(a):
        block = cbuf[tq[a], tn[a]]
        real, imag = block[0], block[1]
        rb, ib = real.astype(BF16), imag.astype(BF16)
        wl[a, 0:BS, 0:BS] = rb
        wl[a, 0:BS, BS:2 * BS] = -ib
        wl[a, BS:2 * BS, 0:BS] = ib
        wl[a, BS:2 * BS, BS:2 * BS] = rb
        rt, it = real.T.astype(BF16), imag.T.astype(BF16)
        wr[a, 0:BS, 0:BS] = rt
        wr[a, 0:BS, BS:2 * BS] = -it
        wr[a, BS:2 * BS, 0:BS] = it
        wr[a, BS:2 * BS, BS:2 * BS] = rt

    @pl.when(jnp.logical_not(has_y))
    def _():
        @pl.loop(0, NCH)
        def _(k):
            ring[k, 4 * c] = jnp.zeros((2, 2, BS, BS), BF16)

    def relay(k):
        r_mate(k)

        @pl.when(y_relay)
        def _():
            c_y(k).start()

        c_relay(k).start()

    relay(0)

    t_up = jnp.where(z == 3, t_swp, t_own)
    t_dn = jnp.where(z == 0, t_swp, t_own)
    w_up = (x == 1).astype(F32)
    w_dn = (x == -1).astype(F32)
    th_swp = ((x == 1) & (z == 3)) | ((x == -1) & (z == 0))

    def sandwich(k, s, six):
        q = qs[s]
        one = sh[q] == 1
        weight = occ[q]
        cols = []
        for e in range(2):
            low = jnp.where(one, six[e + 1], six[e])
            high = jnp.where(one, six[e + 3], six[e + 4])
            mixed = (weight * low.astype(F32) + (weight + 1.0) * high.astype(F32)).astype(BF16)
            cols.append(mixed.reshape(2 * BS, BS))
        field = jnp.concatenate(cols, axis=1)
        left = jnp.dot(wl[s * NB + ti[k]], field, preferred_element_type=F32).astype(BF16)
        top = jnp.concatenate([left[:BS, :BS], left[BS:, :BS]], axis=1)
        bottom = jnp.concatenate([left[:BS, BS:], left[BS:, BS:]], axis=1)
        return jnp.dot(jnp.concatenate([top, bottom], axis=0), wr[s * NB + tj[k]], preferred_element_type=F32)

    def window(k, t):
        return [ring[k, t - 1 + e // 2, e % 2] for e in range(6)]

    def ship(k):
        third = sc[tx[k]]
        snd_p[k] = (sp[...] + w_up * third).astype(BF16)
        snd_m[k] = (sm[...] + w_dn * third).astype(BF16)
        c_up(k).start()
        c_down(k).start()

    @pl.loop(0, NCH)
    def _(k):
        @pl.when(k + 1 < NCH)
        def _():
            relay(k + 1)

        r_relay(k)

        @pl.when(has_y)
        def _():
            r_y(k)

        own = window(k, t_own)
        swp = window(k, t_swp)
        sc[k] = sandwich(k, 2, [jnp.where(th_swp, b, a) for a, b in zip(own, swp)])

        @pl.when(k > 0)
        def _():
            ship(k - 1)

        sp[...] = sandwich(k, 0, window(k, t_up))
        sm[...] = sandwich(k, 1, window(k, t_dn))

    ship(NCH - 1)

    @pl.loop(0, NCH)
    def _(d):
        for s in range(3):
            i = tinv[s * NB + d // NB]
            j = tinv[s * NB + d % NB]
            place = 0
            for k in range(NCH):
                place = jnp.where((ti[k] == i) & (tj[k] == j), k, place)
            if s == 2:
                place = jnp.where(x == 0, place, 0)
            tab[s * NCH + d] = place
    tab[3 * NCH] = (x == 0).astype(jnp.int32)

    def all_sent(n):
        pltpu.make_async_remote_copy(
            snd_p, snd_p, sent.at[n], got.at[0], device_id=partner, device_id_type=MESH).wait_send()

    for n in (0, 1, 2, 4, 5):
        all_sent(n)

    @pl.when(has_y)
    def _():
        all_sent(3)

    arrived(in_p, got.at[0], up)
    arrived(in_m, got.at[1], down)


def gather_sum(tab, in_p, in_m, third, out, rows, sem):
    def copy(r):
        return pltpu.make_async_copy(rows.at[r], out.at[0, :, :, pl.ds(r * BS, BS), :], sem.at[r])

    def fill(own):
        for r in range(NB):
            for j in range(NB):
                d = r * NB + j
                total = in_p[tab[d]].astype(F32) + in_m[tab[NCH + d]].astype(F32)
                if own:
                    total = total + third[tab[2 * NCH + d]]
                for e in range(2):
                    for ri in range(2):
                        rows[r, e, ri, :, j * BS:(j + 1) * BS] = total[e * BS:(e + 1) * BS, ri * BS:(ri + 1) * BS]
            copy(r).start()

    @pl.when(tab[3 * NCH] == 1)
    def _():
        fill(True)

    @pl.when(tab[3 * NCH] != 1)
    def _():
        fill(False)

    for r in range(NB):
        copy(r).wait()


def on_device(green_lesser, coupling, block_list, offsets, shifts, occupation):
    any_spec = pl.BlockSpec(memory_space=pl.ANY)
    hbm = pl.BlockSpec(memory_space=pltpu.HBM)
    smem = pl.BlockSpec(memory_space=pltpu.SMEM)
    vmem = pl.BlockSpec(memory_space=pltpu.VMEM)
    dma = pltpu.SemaphoreType.DMA
    chunk = (NCH, 2 * BS, 2 * BS)
    in_p, in_m, third, tab = pl.pallas_call(
        exchange,
        out_shape=(
            pltpu.VMEM(chunk, BF16),
            pltpu.VMEM(chunk, BF16),
            pltpu.VMEM(chunk, F32),
            pltpu.SMEM((4 * NCH,), jnp.int32),
        ),
        in_specs=[hbm] * 6,
        out_specs=(vmem, vmem, vmem, smem),
        scratch_shapes=[
            pltpu.VMEM((NCH, 2, 2, BS, BS), BF16),
            pltpu.VMEM((3, NB, 2, BS, BS), F32),
            pltpu.VMEM((NCH, 5, 2, 2, BS, BS), BF16),
            pltpu.VMEM((3 * NB, 2 * BS, 2 * BS), BF16),
            pltpu.VMEM((3 * NB, 2 * BS, 2 * BS), BF16),
            pltpu.VMEM((2 * BS, 2 * BS), F32),
            pltpu.VMEM((2 * BS, 2 * BS), F32),
            pltpu.VMEM(chunk, BF16),
            pltpu.VMEM(chunk, BF16),
            pltpu.SMEM((3, 2, NB), jnp.int32),
            pltpu.SMEM((3,), jnp.int32),
            pltpu.SMEM((3,), jnp.int32),
            pltpu.SMEM((3,), F32),
            pltpu.SMEM((3 * NB,), jnp.int32),
            pltpu.SMEM((3 * NB,), jnp.int32),
            pltpu.SMEM((NCH,), jnp.int32),
            pltpu.SMEM((NCH,), jnp.int32),
            pltpu.SMEM((NCH,), jnp.int32),
            pltpu.SMEM((3 * NB,), jnp.int32),
            dma((3,)),
            dma((4,)),
            dma((6,)),
            dma((2,)),
            dma((2,)),
            dma((NCH,)),
            dma((NCH,)),
            dma((NCH,)),
        ],
        compiler_params=pltpu.CompilerParams(
            collective_id=0, has_side_effects=True, vmem_limit_bytes=32 * 1024 * 1024),
        name="exchange",
    )(*(
        pltpu.with_memory_space_constraint(x, pltpu.HBM)
        for x in (green_lesser, coupling, block_list.transpose(0, 2, 1), offsets, shifts, occupation)
    ))
    return pl.pallas_call(
        gather_sum,
        out_shape=jax.ShapeDtypeStruct(green_lesser.shape, F32),
        in_specs=[smem, vmem, vmem, vmem],
        out_specs=any_spec,
        scratch_shapes=[pltpu.VMEM((NB, 2, 2, BS, 512), F32), dma((NB,))],
        compiler_params=pltpu.CompilerParams(vmem_limit_bytes=16 * 1024 * 1024),
        name="gather_sum",
    )(tab, in_p, in_m, third)


def solution(mesh):
    placed = (P("kz", "en", None, None, None), P(), P(), P(), P(), P())
    return jax.shard_map(
        on_device,
        mesh=mesh,
        in_specs=placed,
        out_specs=P("kz", "en", None, None, None),
        check_vma=False,
    )
```

```python
import jax
import jax.numpy as jnp
from jax import lax
from jax.experimental import pallas as pl
from jax.experimental.pallas import tpu as pltpu
from jax.sharding import PartitionSpec as P

MESH = pl.DeviceIdType.MESH
BS = 128
NB = 4
NCH = NB * NB
F32 = jnp.float32
BF16 = jnp.bfloat16


def pick(flags, values):
    *head, chosen = values
    for flag, value in reversed(list(zip(flags, head))):
        chosen = jnp.where(flag, value, chosen)
    return chosen


def exchange(
    g_hbm, cp_hbm, bl_hbm, off_hbm, sh_hbm, occ_hbm,
    in_p, in_m, sc, tab,
    gbuf, cbuf, ring, wl, wr, sp, sm, snd_p, snd_m, bl, off, sh, occ, tq, tn, ti, tj, tx, tinv,
    ready, lsem, isem, sent, got, s1r, s2r, s3r, s4r,
):
    kz = lax.axis_index("kz")
    en = lax.axis_index("en")
    z = kz % 4
    y = en // 4
    lo = (en // 2) % 2
    c = en % 2
    flip = 2 - 4 * lo
    partner = (kz, en + 1 - 2 * c)
    mate = (kz, en + flip)
    has_y = ((c == 1) & (y < 3)) | ((c == 0) & (y > 0))
    yen = (en + 6 * c - 3 + 16) % 16
    ydev = (kz, yen)
    at_top = (z == 3).astype(jnp.int32)
    at_bot = (z == 0).astype(jnp.int32)
    up = ((kz + 1) % 8, en + flip * at_top)
    down = ((kz + 7) % 8, en + flip * at_bot)

    t_own = 1 + 2 * lo
    t_swp = 3 - 2 * lo
    def g_copy(b):
        rows = pl.ds(b // NB * BS, BS)
        columns = pl.ds(b % NB * BS, BS)
        target = ring.at[0, t_own] if b == 0 else gbuf.at[b]
        return pltpu.make_async_copy(g_hbm.at[0, :, :, rows, columns], target, lsem.at[min(b, 1)])

    g_copy(0).start()
    barrier = pltpu.get_barrier_semaphore()

    @pl.when(z < 3)
    def _():
        pl.semaphore_signal(barrier, inc=1, device_id=up, device_id_type=MESH)

    @pl.when(z == 0)
    def _():
        pl.semaphore_signal(barrier, inc=1, device_id=down, device_id_type=MESH)

    for dev in (ydev, mate, partner):
        pl.semaphore_signal(barrier, inc=1, device_id=dev, device_id_type=MESH)
    small = [
        pltpu.make_async_copy(source, target, isem.at[n])
        for n, (source, target) in enumerate(((bl_hbm, bl), (off_hbm, off), (sh_hbm, sh), (occ_hbm, occ)))
    ]
    for copy in small:
        copy.start()
    c_copy = pltpu.make_async_copy(cp_hbm, cbuf, lsem.at[2])

    def c_partner(k, sem):
        return pltpu.make_async_remote_copy(
            ring.at[k, t_own], ring.at[k, 2 * lo + 2 * c], sent.at[0], s1r.at[sem],
            device_id=partner, device_id_type=MESH)

    def c_mate(k):
        return pltpu.make_async_remote_copy(
            ring.at[k, t_own], ring.at[k, t_own], sent.at[1], s2r.at[k], device_id=mate, device_id_type=MESH)

    def c_relay(k):
        return pltpu.make_async_remote_copy(
            ring.at[k, t_swp], ring.at[k, 2 - 2 * lo + 2 * c], sent.at[2], s3r.at[k],
            device_id=partner, device_id_type=MESH)

    def c_y(k):
        return pltpu.make_async_remote_copy(
            ring.at[k, 1 + 2 * c], ring.at[k, 4 - 4 * c], sent.at[3], s4r.at[k], device_id=ydev, device_id_type=MESH)

    def c_up(k):
        return pltpu.make_async_remote_copy(
            snd_p.at[k], in_p.at[k], sent.at[4], got.at[0], device_id=up, device_id_type=MESH)

    def c_down(k):
        return pltpu.make_async_remote_copy(
            snd_m.at[k], in_m.at[k], sent.at[5], got.at[1], device_id=down, device_id_type=MESH)

    def arrived(target, sem, device):
        pltpu.make_async_remote_copy(
            target, target, sent.at[0], sem, device_id=device, device_id_type=MESH).wait_recv()

    def r_mate(k):
        arrived(ring.at[k, t_swp], s2r.at[k], mate)

    def r_relay(k):
        arrived(ring.at[k, 4 - 2 * lo - 2 * c], s3r.at[k], partner)

    def r_y(k):
        arrived(ring.at[k, 4 * c], s4r.at[k], ydev)

    t_partner = 2 * lo + 2 - 2 * c
    y_own = has_y & (lo == c)
    y_relay = has_y & (lo != c)

    def send_mate(k):
        c_mate(k).start()

    def send_chip(k, sem):
        c_partner(k, sem).start()

        @pl.when(y_own)
        def _():
            c_y(k).start()

    g_copy(0).wait()
    pl.semaphore_wait(barrier, 3 + (z > 0).astype(jnp.int32) + at_top)
    send_mate(0)
    send_chip(0, 0)

    @pl.when(z > 0)
    def _():
        pl.semaphore_signal(ready.at[0], inc=1, device_id=down, device_id_type=MESH)

    @pl.when(z == 3)
    def _():
        pl.semaphore_signal(ready.at[1], inc=1, device_id=up, device_id_type=MESH)

    for b in range(1, NCH):
        g_copy(b).start()
    c_copy.start()
    for copy in small:
        copy.wait()

    o0, o1 = off[0], off[1]
    q_up = jnp.where(o0 == 1, 0, jnp.where(o1 == 1, 1, 2))
    q_dn = jnp.where(o0 == -1, 0, jnp.where(o1 == -1, 1, 2))
    q_th = jnp.maximum(3 - q_up - q_dn, 0)
    qs = (q_up, q_dn, q_th)
    x = off[q_th]
    rho = []
    for s, q in enumerate(qs):
        rows = [bl[q, 0, n] for n in range(NB)]
        cols = [bl[q, 1, n] for n in range(NB)]
        dest = []
        for i in range(NB):
            hit = [cols[n] == i for n in range(NB)]
            tq[s * NB + i] = q
            tn[s * NB + i] = pick(hit, range(NB))
            dest.append(pick(hit, rows))
        rho.append(dest)
    inv = [[pick([rho[s][i] == r for i in range(NB)], range(NB)) for r in range(NB)] for s in range(3)]
    for s in range(3):
        for r in range(NB):
            tinv[s * NB + r] = inv[s][r]
    tau = []
    for i in range(NB):
        r = jnp.where(x == 1, rho[0][i], rho[1][i])
        t = pick([r == a for a in range(NB)], inv[2])
        tau.append(jnp.where(x == 0, i, t))
    ci = jnp.int32(0)
    cj = jnp.int32(0)
    start = jnp.int32(0)
    start_k = jnp.int32(0)
    seen = [jnp.bool_(False)] * NCH
    for k in range(NCH):
        ti[k] = ci
        tj[k] = cj
        cur = ci * NB + cj
        seen = [seen[b] | (cur == b) for b in range(NCH)]
        ni = pick([ci == a for a in range(NB)], tau)
        nj = pick([cj == a for a in range(NB)], tau)
        closing = (ni * NB + nj) == start
        tx[k] = jnp.where(closing, start_k, min(k + 1, NCH - 1))
        if k + 1 < NCH:
            free = jnp.int32(NCH - 1)
            for b in reversed(range(NCH - 1)):
                free = jnp.where(seen[b], free, b)
            fi = free // NB
            ci = jnp.where(closing, fi, ni)
            cj = jnp.where(closing, free - fi * NB, nj)
            start = jnp.where(closing, free, start)
            start_k = jnp.where(closing, k + 1, start_k)

    others = gbuf.at[pl.ds(1, NCH - 1)]
    pltpu.make_async_copy(others, others, lsem.at[1]).wait()

    @pl.loop(1, NCH)
    def _(k):
        ring[k, t_own] = gbuf[ti[k] * NB + tj[k]]

        send_mate(k)
        send_chip(k, 1)

    arrived(ring.at[0, t_partner], s1r.at[0], partner)
    arrived(ring.at[pl.ds(1, NCH - 1), t_partner], s1r.at[1], partner)


    c_copy.wait()

    @pl.loop(0, 3 * NB)
    def _(a):
        block = cbuf[tq[a], tn[a]]
        real, imag = block[0], block[1]
        rb, ib = real.astype(BF16), imag.astype(BF16)
        wl[a, 0:BS, 0:BS] = rb
        wl[a, 0:BS, BS:2 * BS] = -ib
        wl[a, BS:2 * BS, 0:BS] = ib
        wl[a, BS:2 * BS, BS:2 * BS] = rb
        rt, it = real.T.astype(BF16), imag.T.astype(BF16)
        wr[a, 0:BS, 0:BS] = rt
        wr[a, 0:BS, BS:2 * BS] = -it
        wr[a, BS:2 * BS, 0:BS] = it
        wr[a, BS:2 * BS, BS:2 * BS] = rt

    @pl.when(jnp.logical_not(has_y))
    def _():
        @pl.loop(0, NCH)
        def _(k):
            ring[k, 4 * c] = jnp.zeros((2, 2, BS, BS), BF16)

    def relay(k):
        r_mate(k)

        @pl.when(y_relay)
        def _():
            c_y(k).start()

        c_relay(k).start()

    relay(0)

    t_up = jnp.where(z == 3, t_swp, t_own)
    t_dn = jnp.where(z == 0, t_swp, t_own)
    w_up = (x == 1).astype(F32)
    w_dn = (x == -1).astype(F32)
    th_swp = ((x == 1) & (z == 3)) | ((x == -1) & (z == 0))

    def sandwich(k, s, six):
        q = qs[s]
        one = sh[q] == 1
        weight = occ[q]
        cols = []
        for e in range(2):
            low = jnp.where(one, six[e + 1], six[e])
            high = jnp.where(one, six[e + 3], six[e + 4])
            mixed = (weight * low.astype(F32) + (weight + 1.0) * high.astype(F32)).astype(BF16)
            cols.append(mixed.reshape(2 * BS, BS))
        field = jnp.concatenate(cols, axis=1)
        left = jnp.dot(wl[s * NB + ti[k]], field, preferred_element_type=F32).astype(BF16)
        top = jnp.concatenate([left[:BS, :BS], left[BS:, :BS]], axis=1)
        bottom = jnp.concatenate([left[:BS, BS:], left[BS:, BS:]], axis=1)
        return jnp.dot(jnp.concatenate([top, bottom], axis=0), wr[s * NB + tj[k]], preferred_element_type=F32)

    def window(k, t):
        return [ring[k, t - 1 + e // 2, e % 2] for e in range(6)]

    def ship(k):
        third = sc[tx[k]]
        snd_p[k] = (sp[...] + w_up * third).astype(BF16)
        snd_m[k] = (sm[...] + w_dn * third).astype(BF16)
        c_up(k).start()
        c_down(k).start()

    @pl.loop(0, NCH)
    def _(k):
        @pl.when(k + 1 < NCH)
        def _():
            relay(k + 1)

        r_relay(k)

        @pl.when(has_y)
        def _():
            r_y(k)

        own = window(k, t_own)
        swp = window(k, t_swp)
        sc[k] = sandwich(k, 2, [jnp.where(th_swp, b, a) for a, b in zip(own, swp)])

        @pl.when((k == 1) & (z < 3))
        def _():
            pl.semaphore_wait(ready.at[0], 1)

        @pl.when((k == 1) & (z == 0))
        def _():
            pl.semaphore_wait(ready.at[1], 1)

        @pl.when(k > 0)
        def _():
            ship(k - 1)

        sp[...] = sandwich(k, 0, window(k, t_up))
        sm[...] = sandwich(k, 1, window(k, t_dn))

    ship(NCH - 1)

    @pl.loop(0, NCH)
    def _(d):
        for s in range(3):
            i = tinv[s * NB + d // NB]
            j = tinv[s * NB + d % NB]
            place = 0
            for k in range(NCH):
                place = jnp.where((ti[k] == i) & (tj[k] == j), k, place)
            if s == 2:
                place = jnp.where(x == 0, place, 0)
            tab[s * NCH + d] = place
    tab[3 * NCH] = (x == 0).astype(jnp.int32)

    def all_sent(n):
        pltpu.make_async_remote_copy(
            snd_p, snd_p, sent.at[n], got.at[0], device_id=partner, device_id_type=MESH).wait_send()

    for n in (0, 1, 2, 4, 5):
        all_sent(n)

    @pl.when(has_y)
    def _():
        all_sent(3)

    arrived(in_p, got.at[0], up)
    arrived(in_m, got.at[1], down)


def gather_sum(tab, in_p, in_m, third, out, rows, sem):
    def copy(r):
        return pltpu.make_async_copy(rows.at[r], out.at[0, :, :, pl.ds(r * BS, BS), :], sem.at[r])

    def fill(own):
        for r in range(NB):
            for j in range(NB):
                d = r * NB + j
                total = in_p[tab[d]].astype(F32) + in_m[tab[NCH + d]].astype(F32)
                if own:
                    total = total + third[tab[2 * NCH + d]]
                for e in range(2):
                    for ri in range(2):
                        rows[r, e, ri, :, j * BS:(j + 1) * BS] = total[e * BS:(e + 1) * BS, ri * BS:(ri + 1) * BS]
            copy(r).start()

    @pl.when(tab[3 * NCH] == 1)
    def _():
        fill(True)

    @pl.when(tab[3 * NCH] != 1)
    def _():
        fill(False)

    for r in range(NB):
        copy(r).wait()


def on_device(green_lesser, coupling, block_list, offsets, shifts, occupation):
    any_spec = pl.BlockSpec(memory_space=pl.ANY)
    hbm = pl.BlockSpec(memory_space=pltpu.HBM)
    smem = pl.BlockSpec(memory_space=pltpu.SMEM)
    vmem = pl.BlockSpec(memory_space=pltpu.VMEM)
    dma = pltpu.SemaphoreType.DMA
    chunk = (NCH, 2 * BS, 2 * BS)
    in_p, in_m, third, tab = pl.pallas_call(
        exchange,
        out_shape=(
            pltpu.VMEM(chunk, BF16),
            pltpu.VMEM(chunk, BF16),
            pltpu.VMEM(chunk, F32),
            pltpu.SMEM((4 * NCH,), jnp.int32),
        ),
        in_specs=[hbm] * 6,
        out_specs=(vmem, vmem, vmem, smem),
        scratch_shapes=[
            pltpu.VMEM((NCH, 2, 2, BS, BS), BF16),
            pltpu.VMEM((3, NB, 2, BS, BS), F32),
            pltpu.VMEM((NCH, 5, 2, 2, BS, BS), BF16),
            pltpu.VMEM((3 * NB, 2 * BS, 2 * BS), BF16),
            pltpu.VMEM((3 * NB, 2 * BS, 2 * BS), BF16),
            pltpu.VMEM((2 * BS, 2 * BS), F32),
            pltpu.VMEM((2 * BS, 2 * BS), F32),
            pltpu.VMEM(chunk, BF16),
            pltpu.VMEM(chunk, BF16),
            pltpu.SMEM((3, 2, NB), jnp.int32),
            pltpu.SMEM((3,), jnp.int32),
            pltpu.SMEM((3,), jnp.int32),
            pltpu.SMEM((3,), F32),
            pltpu.SMEM((3 * NB,), jnp.int32),
            pltpu.SMEM((3 * NB,), jnp.int32),
            pltpu.SMEM((NCH,), jnp.int32),
            pltpu.SMEM((NCH,), jnp.int32),
            pltpu.SMEM((NCH,), jnp.int32),
            pltpu.SMEM((3 * NB,), jnp.int32),
            pltpu.SemaphoreType.REGULAR((2,)),
            dma((3,)),
            dma((4,)),
            dma((6,)),
            dma((2,)),
            dma((2,)),
            dma((NCH,)),
            dma((NCH,)),
            dma((NCH,)),
        ],
        compiler_params=pltpu.CompilerParams(
            collective_id=0, has_side_effects=True, vmem_limit_bytes=32 * 1024 * 1024),
        name="exchange",
    )(*(
        pltpu.with_memory_space_constraint(x, pltpu.HBM)
        for x in (green_lesser, coupling, block_list.transpose(0, 2, 1), offsets, shifts, occupation)
    ))
    return pl.pallas_call(
        gather_sum,
        out_shape=jax.ShapeDtypeStruct(green_lesser.shape, F32),
        in_specs=[smem, vmem, vmem, vmem],
        out_specs=any_spec,
        scratch_shapes=[pltpu.VMEM((NB, 2, 2, BS, 512), F32), dma((NB,))],
        compiler_params=pltpu.CompilerParams(vmem_limit_bytes=16 * 1024 * 1024),
        name="gather_sum",
    )(tab, in_p, in_m, third)


def solution(mesh):
    placed = (P("kz", "en", None, None, None), P(), P(), P(), P(), P())
    return jax.shard_map(
        on_device,
        mesh=mesh,
        in_specs=placed,
        out_specs=P("kz", "en", None, None, None),
        check_vma=False,
    )
```

```python
import jax
import jax.numpy as jnp
from jax import lax
from jax.experimental import pallas as pl
from jax.experimental.pallas import tpu as pltpu
from jax.sharding import PartitionSpec as P

MESH = pl.DeviceIdType.MESH
BS = 128
NB = 4
NCH = NB * NB
F32 = jnp.float32
BF16 = jnp.bfloat16


def pick(flags, values):
    *head, chosen = values
    for flag, value in reversed(list(zip(flags, head))):
        chosen = jnp.where(flag, value, chosen)
    return chosen


def exchange(
    g_hbm, cp_hbm, bl_hbm, off_hbm, sh_hbm, occ_hbm,
    in_p, in_m, sc, tab,
    gbuf, cbuf, ring, wl, wr, sp, sm, snd_p, snd_m, bl, off, sh, occ, tq, tn, ti, tj, tx, tinv,
    ready, lsem, isem, sent, got, s1r, s2r, s3r, s4r,
):
    kz = lax.axis_index("kz")
    en = lax.axis_index("en")
    z = kz % 4
    y = en // 4
    lo = (en // 2) % 2
    c = en % 2
    flip = 2 - 4 * lo
    partner = (kz, en + 1 - 2 * c)
    mate = (kz, en + flip)
    has_y = ((c == 1) & (y < 3)) | ((c == 0) & (y > 0))
    yen = (en + 6 * c - 3 + 16) % 16
    ydev = (kz, yen)
    at_top = (z == 3).astype(jnp.int32)
    at_bot = (z == 0).astype(jnp.int32)
    up = ((kz + 1) % 8, en + flip * at_top)
    down = ((kz + 7) % 8, en + flip * at_bot)

    t_own = 1 + 2 * lo
    t_swp = 3 - 2 * lo
    def g_copy(b):
        rows = pl.ds(b // NB * BS, BS)
        columns = pl.ds(b % NB * BS, BS)
        target = ring.at[0, t_own] if b == 0 else gbuf.at[b]
        return pltpu.make_async_copy(g_hbm.at[0, :, :, rows, columns], target, lsem.at[min(b, 1)])

    g_copy(0).start()
    barrier = pltpu.get_barrier_semaphore()

    @pl.when(z < 3)
    def _():
        pl.semaphore_signal(barrier, inc=1, device_id=up, device_id_type=MESH)

    @pl.when(z == 0)
    def _():
        pl.semaphore_signal(barrier, inc=1, device_id=down, device_id_type=MESH)

    for dev in (ydev, mate, partner):
        pl.semaphore_signal(barrier, inc=1, device_id=dev, device_id_type=MESH)
    small = [
        pltpu.make_async_copy(source, target, isem.at[n])
        for n, (source, target) in enumerate(((bl_hbm, bl), (off_hbm, off), (sh_hbm, sh), (occ_hbm, occ)))
    ]
    for copy in small:
        copy.start()
    c_copy = pltpu.make_async_copy(cp_hbm, cbuf, lsem.at[2])

    def c_partner(k, sem):
        return pltpu.make_async_remote_copy(
            ring.at[k, t_own], ring.at[k, 2 * lo + 2 * c], sent.at[0], s1r.at[sem],
            device_id=partner, device_id_type=MESH)

    def c_mate(k):
        return pltpu.make_async_remote_copy(
            ring.at[k, t_own], ring.at[k, t_own], sent.at[1], s2r.at[k], device_id=mate, device_id_type=MESH)

    def c_relay(k):
        return pltpu.make_async_remote_copy(
            ring.at[k, t_swp], ring.at[k, 2 - 2 * lo + 2 * c], sent.at[2], s3r.at[k],
            device_id=partner, device_id_type=MESH)

    def c_y(k):
        return pltpu.make_async_remote_copy(
            ring.at[k, 1 + 2 * c], ring.at[k, 4 - 4 * c], sent.at[3], s4r.at[k], device_id=ydev, device_id_type=MESH)

    def c_up(k):
        return pltpu.make_async_remote_copy(
            snd_p.at[k], in_p.at[k], sent.at[4], got.at[0], device_id=up, device_id_type=MESH)

    def c_down(k):
        return pltpu.make_async_remote_copy(
            snd_m.at[k], in_m.at[k], sent.at[5], got.at[1], device_id=down, device_id_type=MESH)

    def arrived(target, sem, device):
        pltpu.make_async_remote_copy(
            target, target, sent.at[0], sem, device_id=device, device_id_type=MESH).wait_recv()

    def r_mate(k):
        arrived(ring.at[k, t_swp], s2r.at[k], mate)

    def r_relay(k):
        arrived(ring.at[k, 4 - 2 * lo - 2 * c], s3r.at[k], partner)

    def r_y(k):
        arrived(ring.at[k, 4 * c], s4r.at[k], ydev)

    t_partner = 2 * lo + 2 - 2 * c
    y_own = has_y & (lo == c)
    y_relay = has_y & (lo != c)

    def send_mate(k):
        c_mate(k).start()

    def send_chip(k, sem):
        c_partner(k, sem).start()

        @pl.when(y_own)
        def _():
            c_y(k).start()

    g_copy(0).wait()
    pl.semaphore_wait(barrier, 3 + (z > 0).astype(jnp.int32) + at_top)
    send_mate(0)
    send_chip(0, 0)

    @pl.when(z > 0)
    def _():
        pl.semaphore_signal(ready.at[0], inc=1, device_id=down, device_id_type=MESH)

    @pl.when(z == 3)
    def _():
        pl.semaphore_signal(ready.at[1], inc=1, device_id=up, device_id_type=MESH)

    for b in range(1, NCH):
        g_copy(b).start()
    c_copy.start()
    for copy in small:
        copy.wait()

    o0, o1 = off[0], off[1]
    q_up = jnp.where(o0 == 1, 0, jnp.where(o1 == 1, 1, 2))
    q_dn = jnp.where(o0 == -1, 0, jnp.where(o1 == -1, 1, 2))
    q_th = jnp.maximum(3 - q_up - q_dn, 0)
    qs = (q_up, q_dn, q_th)
    x = off[q_th]
    rho = []
    for s, q in enumerate(qs):
        rows = [bl[q, 0, n] for n in range(NB)]
        cols = [bl[q, 1, n] for n in range(NB)]
        dest = []
        for i in range(NB):
            hit = [cols[n] == i for n in range(NB)]
            tq[s * NB + i] = q
            tn[s * NB + i] = pick(hit, range(NB))
            dest.append(pick(hit, rows))
        rho.append(dest)
    inv = [[pick([rho[s][i] == r for i in range(NB)], range(NB)) for r in range(NB)] for s in range(3)]
    for s in range(3):
        for r in range(NB):
            tinv[s * NB + r] = inv[s][r]
    tau = []
    for i in range(NB):
        r = jnp.where(x == 1, rho[0][i], rho[1][i])
        t = pick([r == a for a in range(NB)], inv[2])
        tau.append(jnp.where(x == 0, i, t))
    ci = jnp.int32(0)
    cj = jnp.int32(0)
    start = jnp.int32(0)
    start_k = jnp.int32(0)
    seen = [jnp.bool_(False)] * NCH
    for k in range(NCH):
        ti[k] = ci
        tj[k] = cj
        cur = ci * NB + cj
        seen = [seen[b] | (cur == b) for b in range(NCH)]
        ni = pick([ci == a for a in range(NB)], tau)
        nj = pick([cj == a for a in range(NB)], tau)
        closing = (ni * NB + nj) == start
        tx[k] = jnp.where(closing, start_k, min(k + 1, NCH - 1))
        if k + 1 < NCH:
            free = jnp.int32(NCH - 1)
            for b in reversed(range(NCH - 1)):
                free = jnp.where(seen[b], free, b)
            fi = free // NB
            ci = jnp.where(closing, fi, ni)
            cj = jnp.where(closing, free - fi * NB, nj)
            start = jnp.where(closing, free, start)
            start_k = jnp.where(closing, k + 1, start_k)

    others = gbuf.at[pl.ds(1, NCH - 1)]
    pltpu.make_async_copy(others, others, lsem.at[1]).wait()

    @pl.loop(1, NCH)
    def _(k):
        ring[k, t_own] = gbuf[ti[k] * NB + tj[k]]

        send_mate(k)
        send_chip(k, 1)


    def relay(k):
        r_mate(k)

        @pl.when(y_relay)
        def _():
            c_y(k).start()

        c_relay(k).start()

    relay(0)
    c_copy.wait()

    @pl.loop(0, 3 * NB)
    def _(a):
        block = cbuf[tq[a], tn[a]]
        real, imag = block[0], block[1]
        rb, ib = real.astype(BF16), imag.astype(BF16)
        wl[a, 0:BS, 0:BS] = rb
        wl[a, 0:BS, BS:2 * BS] = -ib
        wl[a, BS:2 * BS, 0:BS] = ib
        wl[a, BS:2 * BS, BS:2 * BS] = rb
        rt, it = real.T.astype(BF16), imag.T.astype(BF16)
        wr[a, 0:BS, 0:BS] = rt
        wr[a, 0:BS, BS:2 * BS] = -it
        wr[a, BS:2 * BS, 0:BS] = it
        wr[a, BS:2 * BS, BS:2 * BS] = rt

    @pl.when(jnp.logical_not(has_y))
    def _():
        @pl.loop(0, NCH)
        def _(k):
            ring[k, 4 * c] = jnp.zeros((2, 2, BS, BS), BF16)


    t_up = jnp.where(z == 3, t_swp, t_own)
    t_dn = jnp.where(z == 0, t_swp, t_own)
    w_up = (x == 1).astype(F32)
    w_dn = (x == -1).astype(F32)
    th_swp = ((x == 1) & (z == 3)) | ((x == -1) & (z == 0))

    def sandwich(k, s, six):
        q = qs[s]
        one = sh[q] == 1
        weight = occ[q]
        cols = []
        for e in range(2):
            low = jnp.where(one, six[e + 1], six[e])
            high = jnp.where(one, six[e + 3], six[e + 4])
            mixed = (weight * low.astype(F32) + (weight + 1.0) * high.astype(F32)).astype(BF16)
            cols.append(mixed.reshape(2 * BS, BS))
        field = jnp.concatenate(cols, axis=1)
        left = jnp.dot(wl[s * NB + ti[k]], field, preferred_element_type=F32).astype(BF16)
        top = jnp.concatenate([left[:BS, :BS], left[BS:, :BS]], axis=1)
        bottom = jnp.concatenate([left[:BS, BS:], left[BS:, BS:]], axis=1)
        return jnp.dot(jnp.concatenate([top, bottom], axis=0), wr[s * NB + tj[k]], preferred_element_type=F32)

    def window(k, t):
        return [ring[k, t - 1 + e // 2, e % 2] for e in range(6)]

    def ship(k):
        third = sc[tx[k]]
        snd_p[k] = (sp[...] + w_up * third).astype(BF16)
        c_up(k).start()
        snd_m[k] = (sm[...] + w_dn * third).astype(BF16)
        c_down(k).start()

    @pl.loop(0, NCH)
    def _(k):
        @pl.when(k + 1 < NCH)
        def _():
            relay(k + 1)

        @pl.when(k == 0)
        def _():
            arrived(ring.at[0, t_partner], s1r.at[0], partner)

        @pl.when(k == 1)
        def _():
            arrived(ring.at[pl.ds(1, NCH - 1), t_partner], s1r.at[1], partner)

        r_relay(k)

        @pl.when(has_y)
        def _():
            r_y(k)

        own = window(k, t_own)
        swp = window(k, t_swp)
        sc[k] = sandwich(k, 2, [jnp.where(th_swp, b, a) for a, b in zip(own, swp)])

        @pl.when((k == 1) & (z < 3))
        def _():
            pl.semaphore_wait(ready.at[0], 1)

        @pl.when((k == 1) & (z == 0))
        def _():
            pl.semaphore_wait(ready.at[1], 1)

        @pl.when(k > 0)
        def _():
            ship(k - 1)

        sp[...] = sandwich(k, 0, window(k, t_up))
        sm[...] = sandwich(k, 1, window(k, t_dn))

    ship(NCH - 1)

    @pl.loop(0, NCH)
    def _(d):
        for s in range(3):
            i = tinv[s * NB + d // NB]
            j = tinv[s * NB + d % NB]
            place = 0
            for k in range(NCH):
                place = jnp.where((ti[k] == i) & (tj[k] == j), k, place)
            if s == 2:
                place = jnp.where(x == 0, place, 0)
            tab[s * NCH + d] = place
    tab[3 * NCH] = (x == 0).astype(jnp.int32)

    def all_sent(n):
        pltpu.make_async_remote_copy(
            snd_p, snd_p, sent.at[n], got.at[0], device_id=partner, device_id_type=MESH).wait_send()

    for n in (0, 1, 2, 4, 5):
        all_sent(n)

    @pl.when(has_y)
    def _():
        all_sent(3)

    arrived(in_p, got.at[0], up)
    arrived(in_m, got.at[1], down)


def gather_sum(tab, in_p, in_m, third, out, rows, sem):
    def copy(d):
        place = out.at[0, :, :, pl.ds(d // NB * BS, BS), pl.ds(d % NB * BS, BS)]
        return pltpu.make_async_copy(rows.at[d], place, sem.at[0])

    def fill(own):
        for r in range(NB):
            for j in range(NB):
                d = r * NB + j
                total = in_p[tab[d]].astype(F32) + in_m[tab[NCH + d]].astype(F32)
                if own:
                    total = total + third[tab[2 * NCH + d]]
                for e in range(2):
                    for ri in range(2):
                        rows[d, e, ri] = total[e * BS:(e + 1) * BS, ri * BS:(ri + 1) * BS]
                copy(d).start()

    @pl.when(tab[3 * NCH] == 1)
    def _():
        fill(True)

    @pl.when(tab[3 * NCH] != 1)
    def _():
        fill(False)

    pltpu.make_async_copy(rows, rows, sem.at[0]).wait()


def on_device(green_lesser, coupling, block_list, offsets, shifts, occupation):
    any_spec = pl.BlockSpec(memory_space=pl.ANY)
    hbm = pl.BlockSpec(memory_space=pltpu.HBM)
    smem = pl.BlockSpec(memory_space=pltpu.SMEM)
    vmem = pl.BlockSpec(memory_space=pltpu.VMEM)
    dma = pltpu.SemaphoreType.DMA
    chunk = (NCH, 2 * BS, 2 * BS)
    in_p, in_m, third, tab = pl.pallas_call(
        exchange,
        out_shape=(
            pltpu.VMEM(chunk, BF16),
            pltpu.VMEM(chunk, BF16),
            pltpu.VMEM(chunk, F32),
            pltpu.SMEM((4 * NCH,), jnp.int32),
        ),
        in_specs=[hbm] * 6,
        out_specs=(vmem, vmem, vmem, smem),
        scratch_shapes=[
            pltpu.VMEM((NCH, 2, 2, BS, BS), BF16),
            pltpu.VMEM((3, NB, 2, BS, BS), F32),
            pltpu.VMEM((NCH, 5, 2, 2, BS, BS), BF16),
            pltpu.VMEM((3 * NB, 2 * BS, 2 * BS), BF16),
            pltpu.VMEM((3 * NB, 2 * BS, 2 * BS), BF16),
            pltpu.VMEM((2 * BS, 2 * BS), F32),
            pltpu.VMEM((2 * BS, 2 * BS), F32),
            pltpu.VMEM(chunk, BF16),
            pltpu.VMEM(chunk, BF16),
            pltpu.SMEM((3, 2, NB), jnp.int32),
            pltpu.SMEM((3,), jnp.int32),
            pltpu.SMEM((3,), jnp.int32),
            pltpu.SMEM((3,), F32),
            pltpu.SMEM((3 * NB,), jnp.int32),
            pltpu.SMEM((3 * NB,), jnp.int32),
            pltpu.SMEM((NCH,), jnp.int32),
            pltpu.SMEM((NCH,), jnp.int32),
            pltpu.SMEM((NCH,), jnp.int32),
            pltpu.SMEM((3 * NB,), jnp.int32),
            pltpu.SemaphoreType.REGULAR((2,)),
            dma((3,)),
            dma((4,)),
            dma((6,)),
            dma((2,)),
            dma((2,)),
            dma((NCH,)),
            dma((NCH,)),
            dma((NCH,)),
        ],
        compiler_params=pltpu.CompilerParams(
            collective_id=0, has_side_effects=True, vmem_limit_bytes=32 * 1024 * 1024),
        name="exchange",
    )(*(
        pltpu.with_memory_space_constraint(x, pltpu.HBM)
        for x in (green_lesser, coupling, block_list.transpose(0, 2, 1), offsets, shifts, occupation)
    ))
    return pl.pallas_call(
        gather_sum,
        out_shape=jax.ShapeDtypeStruct(green_lesser.shape, F32),
        in_specs=[smem, vmem, vmem, vmem],
        out_specs=any_spec,
        scratch_shapes=[pltpu.VMEM((NCH, 2, 2, BS, BS), F32), dma((1,))],
        compiler_params=pltpu.CompilerParams(vmem_limit_bytes=16 * 1024 * 1024),
        name="gather_sum",
    )(tab, in_p, in_m, third)


def solution(mesh):
    placed = (P("kz", "en", None, None, None), P(), P(), P(), P(), P())
    return jax.shard_map(
        on_device,
        mesh=mesh,
        in_specs=placed,
        out_specs=P("kz", "en", None, None, None),
        check_vma=False,
    )
```

```python
import jax
import jax.numpy as jnp
from jax import lax
from jax.experimental import pallas as pl
from jax.experimental.pallas import tpu as pltpu
from jax.sharding import PartitionSpec as P

MESH = pl.DeviceIdType.MESH
BS = 128
NB = 4
NCH = NB * NB
F32 = jnp.float32
BF16 = jnp.bfloat16


def pick(flags, values):
    *head, chosen = values
    for flag, value in reversed(list(zip(flags, head))):
        chosen = jnp.where(flag, value, chosen)
    return chosen


def exchange(
    g_hbm, cp_hbm, bl_hbm, off_hbm, sh_hbm, occ_hbm,
    in_p, in_m, sc, tab,
    gbuf, cbuf, ring, wl, wr, sp, sm, snd_p, snd_m, bl, off, sh, occ, tq, tn, ti, tj, tx, tinv,
    ready, lsem, isem, sent, got, s1r, s2r, s3r, s4r,
):
    kz = lax.axis_index("kz")
    en = lax.axis_index("en")
    z = kz % 4
    y = en // 4
    lo = (en // 2) % 2
    c = en % 2
    flip = 2 - 4 * lo
    partner = (kz, en + 1 - 2 * c)
    mate = (kz, en + flip)
    has_y = ((c == 1) & (y < 3)) | ((c == 0) & (y > 0))
    yen = (en + 6 * c - 3 + 16) % 16
    ydev = (kz, yen)
    at_top = (z == 3).astype(jnp.int32)
    at_bot = (z == 0).astype(jnp.int32)
    up = ((kz + 1) % 8, en + flip * at_top)
    down = ((kz + 7) % 8, en + flip * at_bot)

    t_own = 1 + 2 * lo
    t_swp = 3 - 2 * lo
    def g_copy(b):
        rows = pl.ds(b // NB * BS, BS)
        columns = pl.ds(b % NB * BS, BS)
        target = ring.at[0, t_own] if b == 0 else gbuf.at[b]
        return pltpu.make_async_copy(g_hbm.at[0, :, :, rows, columns], target, lsem.at[min(b, 1)])

    g_copy(0).start()
    barrier = pltpu.get_barrier_semaphore()

    @pl.when(z < 3)
    def _():
        pl.semaphore_signal(barrier, inc=1, device_id=up, device_id_type=MESH)

    @pl.when(z == 0)
    def _():
        pl.semaphore_signal(barrier, inc=1, device_id=down, device_id_type=MESH)

    for dev in (ydev, mate, partner):
        pl.semaphore_signal(barrier, inc=1, device_id=dev, device_id_type=MESH)
    small = [
        pltpu.make_async_copy(source, target, isem.at[n])
        for n, (source, target) in enumerate(((bl_hbm, bl), (off_hbm, off), (sh_hbm, sh), (occ_hbm, occ)))
    ]
    for copy in small:
        copy.start()
    c_copy = pltpu.make_async_copy(cp_hbm, cbuf, lsem.at[2])

    def c_partner(k, sem):
        return pltpu.make_async_remote_copy(
            ring.at[k, t_own], ring.at[k, 2 * lo + 2 * c], sent.at[0], s1r.at[sem],
            device_id=partner, device_id_type=MESH)

    def c_mate(k, h):
        return pltpu.make_async_remote_copy(
            ring.at[k, t_own, h], ring.at[k, t_own, h], sent.at[1], s2r.at[k, h],
            device_id=mate, device_id_type=MESH)

    def c_relay(k):
        return pltpu.make_async_remote_copy(
            ring.at[k, t_swp], ring.at[k, 2 - 2 * lo + 2 * c], sent.at[2], s3r.at[k],
            device_id=partner, device_id_type=MESH)

    def c_y(k, h):
        return pltpu.make_async_remote_copy(
            ring.at[k, 1 + 2 * c, h], ring.at[k, 4 - 4 * c, h], sent.at[3], s4r.at[k, h],
            device_id=ydev, device_id_type=MESH)

    def c_up(k):
        return pltpu.make_async_remote_copy(
            snd_p.at[k], in_p.at[k], sent.at[4], got.at[0], device_id=up, device_id_type=MESH)

    def c_down(k):
        return pltpu.make_async_remote_copy(
            snd_m.at[k], in_m.at[k], sent.at[5], got.at[1], device_id=down, device_id_type=MESH)

    def arrived(target, sem, device):
        pltpu.make_async_remote_copy(
            target, target, sent.at[0], sem, device_id=device, device_id_type=MESH).wait_recv()

    def r_mate(k, h):
        arrived(ring.at[k, t_swp, h], s2r.at[k, h], mate)

    def r_relay(k):
        arrived(ring.at[k, 4 - 2 * lo - 2 * c], s3r.at[k], partner)

    def r_y(k):
        for h in range(2):
            arrived(ring.at[k, 4 * c, h], s4r.at[k, h], ydev)

    t_partner = 2 * lo + 2 - 2 * c
    y_own = has_y & (lo == c)
    y_relay = has_y & (lo != c)

    def send_mate(k):
        for h in range(2):
            c_mate(k, h).start()

    def send_chip(k, sem):
        c_partner(k, sem).start()

        @pl.when(y_own)
        def _():
            for h in range(2):
                c_y(k, h).start()

    g_copy(0).wait()
    pl.semaphore_wait(barrier, 3 + (z > 0).astype(jnp.int32) + at_top)
    send_mate(0)
    send_chip(0, 0)

    @pl.when(z > 0)
    def _():
        pl.semaphore_signal(ready.at[0], inc=1, device_id=down, device_id_type=MESH)

    @pl.when(z == 3)
    def _():
        pl.semaphore_signal(ready.at[1], inc=1, device_id=up, device_id_type=MESH)

    for b in range(1, NCH):
        g_copy(b).start()
    c_copy.start()
    for copy in small:
        copy.wait()

    o0, o1 = off[0], off[1]
    q_up = jnp.where(o0 == 1, 0, jnp.where(o1 == 1, 1, 2))
    q_dn = jnp.where(o0 == -1, 0, jnp.where(o1 == -1, 1, 2))
    q_th = jnp.maximum(3 - q_up - q_dn, 0)
    qs = (q_up, q_dn, q_th)
    x = off[q_th]
    rho = []
    for s, q in enumerate(qs):
        rows = [bl[q, 0, n] for n in range(NB)]
        cols = [bl[q, 1, n] for n in range(NB)]
        dest = []
        for i in range(NB):
            hit = [cols[n] == i for n in range(NB)]
            tq[s * NB + i] = q
            tn[s * NB + i] = pick(hit, range(NB))
            dest.append(pick(hit, rows))
        rho.append(dest)
    inv = [[pick([rho[s][i] == r for i in range(NB)], range(NB)) for r in range(NB)] for s in range(3)]
    for s in range(3):
        for r in range(NB):
            tinv[s * NB + r] = inv[s][r]
    tau = []
    for i in range(NB):
        r = jnp.where(x == 1, rho[0][i], rho[1][i])
        t = pick([r == a for a in range(NB)], inv[2])
        tau.append(jnp.where(x == 0, i, t))
    ci = jnp.int32(0)
    cj = jnp.int32(0)
    start = jnp.int32(0)
    start_k = jnp.int32(0)
    seen = [jnp.bool_(False)] * NCH
    for k in range(NCH):
        ti[k] = ci
        tj[k] = cj
        cur = ci * NB + cj
        seen = [seen[b] | (cur == b) for b in range(NCH)]
        ni = pick([ci == a for a in range(NB)], tau)
        nj = pick([cj == a for a in range(NB)], tau)
        closing = (ni * NB + nj) == start
        tx[k] = jnp.where(closing, start_k, min(k + 1, NCH - 1))
        if k + 1 < NCH:
            free = jnp.int32(NCH - 1)
            for b in reversed(range(NCH - 1)):
                free = jnp.where(seen[b], free, b)
            fi = free // NB
            ci = jnp.where(closing, fi, ni)
            cj = jnp.where(closing, free - fi * NB, nj)
            start = jnp.where(closing, free, start)
            start_k = jnp.where(closing, k + 1, start_k)

    others = gbuf.at[pl.ds(1, NCH - 1)]
    pltpu.make_async_copy(others, others, lsem.at[1]).wait()

    @pl.loop(1, NCH)
    def _(k):
        ring[k, t_own] = gbuf[ti[k] * NB + tj[k]]

        send_mate(k)
        send_chip(k, 1)


    def relay(k):
        for h in range(2):
            r_mate(k, h)

            @pl.when(y_relay)
            def _():
                c_y(k, h).start()

        c_relay(k).start()

    relay(0)
    c_copy.wait()

    @pl.loop(0, 3 * NB)
    def _(a):
        block = cbuf[tq[a], tn[a]]
        real, imag = block[0], block[1]
        rb, ib = real.astype(BF16), imag.astype(BF16)
        wl[a, 0:BS, 0:BS] = rb
        wl[a, 0:BS, BS:2 * BS] = -ib
        wl[a, BS:2 * BS, 0:BS] = ib
        wl[a, BS:2 * BS, BS:2 * BS] = rb
        rt, it = real.T.astype(BF16), imag.T.astype(BF16)
        wr[a, 0:BS, 0:BS] = rt
        wr[a, 0:BS, BS:2 * BS] = -it
        wr[a, BS:2 * BS, 0:BS] = it
        wr[a, BS:2 * BS, BS:2 * BS] = rt

    @pl.when(jnp.logical_not(has_y))
    def _():
        @pl.loop(0, NCH)
        def _(k):
            ring[k, 4 * c] = jnp.zeros((2, 2, BS, BS), BF16)


    t_up = jnp.where(z == 3, t_swp, t_own)
    t_dn = jnp.where(z == 0, t_swp, t_own)
    w_up = (x == 1).astype(F32)
    w_dn = (x == -1).astype(F32)
    th_swp = ((x == 1) & (z == 3)) | ((x == -1) & (z == 0))

    def sandwich(k, s, six):
        q = qs[s]
        one = sh[q] == 1
        weight = occ[q]
        cols = []
        for e in range(2):
            low = jnp.where(one, six[e + 1], six[e])
            high = jnp.where(one, six[e + 3], six[e + 4])
            mixed = (weight * low.astype(F32) + (weight + 1.0) * high.astype(F32)).astype(BF16)
            cols.append(mixed.reshape(2 * BS, BS))
        field = jnp.concatenate(cols, axis=1)
        left = jnp.dot(wl[s * NB + ti[k]], field, preferred_element_type=F32).astype(BF16)
        top = jnp.concatenate([left[:BS, :BS], left[BS:, :BS]], axis=1)
        bottom = jnp.concatenate([left[:BS, BS:], left[BS:, BS:]], axis=1)
        return jnp.dot(jnp.concatenate([top, bottom], axis=0), wr[s * NB + tj[k]], preferred_element_type=F32)

    def window(k, t):
        return [ring[k, t - 1 + e // 2, e % 2] for e in range(6)]

    def ship(k):
        third = sc[tx[k]]
        snd_p[k] = (sp[...] + w_up * third).astype(BF16)
        c_up(k).start()
        snd_m[k] = (sm[...] + w_dn * third).astype(BF16)
        c_down(k).start()

    @pl.loop(0, NCH)
    def _(k):
        @pl.when(k + 1 < NCH)
        def _():
            relay(k + 1)

        @pl.when(k == 0)
        def _():
            arrived(ring.at[0, t_partner], s1r.at[0], partner)

        @pl.when(k == 1)
        def _():
            arrived(ring.at[pl.ds(1, NCH - 1), t_partner], s1r.at[1], partner)

        r_relay(k)

        @pl.when(has_y)
        def _():
            r_y(k)

        own = window(k, t_own)
        swp = window(k, t_swp)
        sc[k] = sandwich(k, 2, [jnp.where(th_swp, b, a) for a, b in zip(own, swp)])

        @pl.when((k == 1) & (z < 3))
        def _():
            pl.semaphore_wait(ready.at[0], 1)

        @pl.when((k == 1) & (z == 0))
        def _():
            pl.semaphore_wait(ready.at[1], 1)

        @pl.when(k > 0)
        def _():
            ship(k - 1)

        sp[...] = sandwich(k, 0, window(k, t_up))
        sm[...] = sandwich(k, 1, window(k, t_dn))

    ship(NCH - 1)

    @pl.loop(0, NCH)
    def _(d):
        for s in range(3):
            i = tinv[s * NB + d // NB]
            j = tinv[s * NB + d % NB]
            place = 0
            for k in range(NCH):
                place = jnp.where((ti[k] == i) & (tj[k] == j), k, place)
            if s == 2:
                place = jnp.where(x == 0, place, 0)
            tab[s * NCH + d] = place
    tab[3 * NCH] = (x == 0).astype(jnp.int32)

    def all_sent(n):
        pltpu.make_async_remote_copy(
            snd_p, snd_p, sent.at[n], got.at[0], device_id=partner, device_id_type=MESH).wait_send()

    for n in (0, 1, 2, 4, 5):
        all_sent(n)

    @pl.when(has_y)
    def _():
        all_sent(3)

    arrived(in_p, got.at[0], up)
    arrived(in_m, got.at[1], down)


def gather_sum(tab, in_p, in_m, third, out, rows, sem):
    def copy(d):
        place = out.at[0, :, :, pl.ds(d // NB * BS, BS), pl.ds(d % NB * BS, BS)]
        return pltpu.make_async_copy(rows.at[d], place, sem.at[0])

    def fill(own):
        for r in range(NB):
            for j in range(NB):
                d = r * NB + j
                total = in_p[tab[d]].astype(F32) + in_m[tab[NCH + d]].astype(F32)
                if own:
                    total = total + third[tab[2 * NCH + d]]
                for e in range(2):
                    for ri in range(2):
                        rows[d, e, ri] = total[e * BS:(e + 1) * BS, ri * BS:(ri + 1) * BS]
                copy(d).start()

    @pl.when(tab[3 * NCH] == 1)
    def _():
        fill(True)

    @pl.when(tab[3 * NCH] != 1)
    def _():
        fill(False)

    pltpu.make_async_copy(rows, rows, sem.at[0]).wait()


def on_device(green_lesser, coupling, block_list, offsets, shifts, occupation):
    any_spec = pl.BlockSpec(memory_space=pl.ANY)
    hbm = pl.BlockSpec(memory_space=pltpu.HBM)
    smem = pl.BlockSpec(memory_space=pltpu.SMEM)
    vmem = pl.BlockSpec(memory_space=pltpu.VMEM)
    dma = pltpu.SemaphoreType.DMA
    chunk = (NCH, 2 * BS, 2 * BS)
    in_p, in_m, third, tab = pl.pallas_call(
        exchange,
        out_shape=(
            pltpu.VMEM(chunk, BF16),
            pltpu.VMEM(chunk, BF16),
            pltpu.VMEM(chunk, F32),
            pltpu.SMEM((4 * NCH,), jnp.int32),
        ),
        in_specs=[hbm] * 6,
        out_specs=(vmem, vmem, vmem, smem),
        scratch_shapes=[
            pltpu.VMEM((NCH, 2, 2, BS, BS), BF16),
            pltpu.VMEM((3, NB, 2, BS, BS), F32),
            pltpu.VMEM((NCH, 5, 2, 2, BS, BS), BF16),
            pltpu.VMEM((3 * NB, 2 * BS, 2 * BS), BF16),
            pltpu.VMEM((3 * NB, 2 * BS, 2 * BS), BF16),
            pltpu.VMEM((2 * BS, 2 * BS), F32),
            pltpu.VMEM((2 * BS, 2 * BS), F32),
            pltpu.VMEM(chunk, BF16),
            pltpu.VMEM(chunk, BF16),
            pltpu.SMEM((3, 2, NB), jnp.int32),
            pltpu.SMEM((3,), jnp.int32),
            pltpu.SMEM((3,), jnp.int32),
            pltpu.SMEM((3,), F32),
            pltpu.SMEM((3 * NB,), jnp.int32),
            pltpu.SMEM((3 * NB,), jnp.int32),
            pltpu.SMEM((NCH,), jnp.int32),
            pltpu.SMEM((NCH,), jnp.int32),
            pltpu.SMEM((NCH,), jnp.int32),
            pltpu.SMEM((3 * NB,), jnp.int32),
            pltpu.SemaphoreType.REGULAR((2,)),
            dma((3,)),
            dma((4,)),
            dma((6,)),
            dma((2,)),
            dma((2,)),
            dma((NCH, 2)),
            dma((NCH,)),
            dma((NCH, 2)),
        ],
        compiler_params=pltpu.CompilerParams(
            collective_id=0, has_side_effects=True, vmem_limit_bytes=32 * 1024 * 1024),
        name="exchange",
    )(*(
        pltpu.with_memory_space_constraint(x, pltpu.HBM)
        for x in (green_lesser, coupling, block_list.transpose(0, 2, 1), offsets, shifts, occupation)
    ))
    return pl.pallas_call(
        gather_sum,
        out_shape=jax.ShapeDtypeStruct(green_lesser.shape, F32),
        in_specs=[smem, vmem, vmem, vmem],
        out_specs=any_spec,
        scratch_shapes=[pltpu.VMEM((NCH, 2, 2, BS, BS), F32), dma((1,))],
        compiler_params=pltpu.CompilerParams(vmem_limit_bytes=16 * 1024 * 1024),
        name="gather_sum",
    )(tab, in_p, in_m, third)


def solution(mesh):
    placed = (P("kz", "en", None, None, None), P(), P(), P(), P(), P())
    return jax.shard_map(
        on_device,
        mesh=mesh,
        in_specs=placed,
        out_specs=P("kz", "en", None, None, None),
        check_vma=False,
    )
```
